32 devices in a mesh: grp: 2 (over y), wide: 8 (over z, x), narrow: 2 (over core).
Axes of the slice: x: 2, y: 2, z: 4, core: 2. Of those that a mesh axis runs over, the one named last changes fastest.
Arguments:
- node_latent: bfloat16 [5120, 512], P(('grp', 'wide', 'narrow')), parts along dimension 0, may hold values from -6 to 6
- fine_edges: bfloat16 [30720, 512], P(('grp', 'wide', 'narrow')), parts along dimension 0, may hold values from -6 to 6
- fine_senders: int32 [30720], P(('grp', 'wide', 'narrow')), parts along dimension 0, may hold values from 0 to 2559, as said below
- fine_receivers: int32 [30720], P(('grp', 'wide', 'narrow')), parts along dimension 0, may hold values from 0 to 2559, as said below
- coarse_edges: bfloat16 [1024, 512], P(('grp', 'wide', 'narrow')), parts along dimension 0, may hold values from -6 to 6
- coarse_senders: int32 [1024], P(('grp', 'wide', 'narrow')), parts along dimension 0, may hold values from 0 to 2403, as said below
- coarse_receivers: int32 [1024], P(('grp', 'wide', 'narrow')), parts along dimension 0, may hold values from 0 to 2403, as said below
- edge_weight_in: bfloat16 [1536, 512], replicated, may hold values from -0.15625 to 0.15625
- edge_bias: float32 [512], replicated, may hold values from -3 to 3
- edge_weight_out: bfloat16 [512, 512], replicated, may hold values from -0.25 to 0.25
- edge_gain: float32 [512], replicated, may hold values from 0.5 to 1.5
- edge_shift: float32 [512], replicated, may hold values from -2 to 2
- node_weight_in: bfloat16 [1024, 512], replicated, may hold values from -0.1875 to 0.1875
- node_bias: float32 [512], replicated, may hold values from -3 to 3
- node_weight_out: bfloat16 [512, 512], replicated, may hold values from -0.25 to 0.25
- node_gain: float32 [512], replicated, may hold values from 0.5 to 1.5
- node_shift: float32 [512], replicated, may hold values from -2 to 2
Outputs:
- node_out: bfloat16 [5120, 512], P(('grp', 'wide', 'narrow')), parts along dimension 0
The draws below stay inside these ranges and needn't reach their ends.
There are 2 independent parts, one for each index of `grp`. The reference program is written for one: setup_inputs(seed, part) draws one part's arguments, and reference() takes and returns one part's arrays. A program takes and returns all parts, laid end to end along the dimension named above; an argument that names none is the same for every part. Nothing has to cross between parts.
Inputs may be any that keep to these rules, and one draw needn't show every extreme that they name: `fine_receivers`: node v belongs to device v // 160 (devices numbered wide index times 2 plus narrow index) and to patch v // 320. Each block of 960 fine edges belongs to one device, in order, and its receivers are that device's nodes. `fine_senders`: the sender of a fine edge lies in the receiver's patch p, or is a boundary node (v % 160 >= 140) of a device of patch p - 1 or p + 1, modulo 8. `coarse_receivers`: coarse nodes are the nodes v with v % 160 < 4. Each block of 32 coarse edges belongs to one device, in order, and its receivers are that device's coarse nodes; each coarse node receives at least one. `coarse_senders`: every coarse sender is a coarse node, on any device.
All inputs are finite; a program needn't handle non-finite values.
Results may differ from the reference program's by a relative error of at most 0.0053.
Values may be sent and summed in bfloat16 or wider, within the bound.
No kernel may reach another device: no remote copies, remote signals or barrier semaphores. Data moves between devices by JAX's collectives and lax.ppermute only.
A program may use at most 64 MiB of HBM per device.

```python
import jax
import jax.numpy as jnp
from jax import lax

D = 512
NODE_DEV = 160
FAN = 6
COARSE_DEV = 4
COARSE_FAN = 8
HALO = 20
PATCHES = 8
PATCH = 320
NODES = 2560
FINE_EDGES = 15360
COARSE_EDGES = 512


def build_graph(key):
    devices = NODES // NODE_DEV
    narrow_count = PATCH // NODE_DEV
    keys = jax.random.split(jax.random.fold_in(key, 7001), 11)
    fine_block = FAN * NODE_DEV
    edge_index = jnp.arange(FINE_EDGES, dtype=jnp.int32)
    owner = edge_index // fine_block
    within = edge_index % fine_block
    loose = jax.random.randint(keys[1], (FINE_EDGES,), 0, NODE_DEV, dtype=jnp.int32)
    recv_local = jnp.where(within < (FAN - 2) * NODE_DEV, within % NODE_DEV, loose)
    fine_receivers = owner * NODE_DEV + recv_local
    patch_index = owner // narrow_count
    across = jax.random.randint(keys[2], (FINE_EDGES,), 0, 8, dtype=jnp.int32) == 0
    side = jax.random.randint(keys[3], (FINE_EDGES,), 0, 2, dtype=jnp.int32) * 2 - 1
    other = (patch_index + side) % PATCHES * narrow_count + jax.random.randint(keys[4], (FINE_EDGES,), 0, narrow_count, dtype=jnp.int32)
    chosen = jax.random.randint(keys[5], (FINE_EDGES,), 0, HALO, dtype=jnp.int32)
    remote = other * NODE_DEV + (NODE_DEV - HALO) + chosen
    inner = patch_index * PATCH + jax.random.randint(keys[6], (FINE_EDGES,), 0, PATCH, dtype=jnp.int32)
    fine_senders = jnp.where(across, remote, inner)
    coarse_block = COARSE_FAN * COARSE_DEV
    coarse_index = jnp.arange(COARSE_EDGES, dtype=jnp.int32)
    coarse_owner = coarse_index // coarse_block
    coarse_within = coarse_index % coarse_block
    skewed = jnp.minimum(jax.random.randint(keys[7], (COARSE_EDGES,), 0, COARSE_DEV, dtype=jnp.int32), jax.random.randint(keys[8], (COARSE_EDGES,), 0, COARSE_DEV, dtype=jnp.int32))
    coarse_local = jnp.where(coarse_within < COARSE_DEV, coarse_within, skewed)
    coarse_receivers = coarse_owner * NODE_DEV + coarse_local
    anywhere = jax.random.randint(keys[9], (COARSE_EDGES,), 0, devices, dtype=jnp.int32)
    opposite = (coarse_owner + devices // 2) % devices
    sender_device = jnp.where(coarse_within % 2 == 0, opposite, anywhere)
    coarse_senders = sender_device * NODE_DEV + jax.random.randint(keys[10], (COARSE_EDGES,), 0, COARSE_DEV, dtype=jnp.int32)
    return (fine_senders, fine_receivers, coarse_senders, coarse_receivers)


def draw_fine_senders(key, part):
    return build_graph(key)[0]


def draw_fine_receivers(key, part):
    return build_graph(key)[1]


def draw_coarse_senders(key, part):
    return build_graph(key)[2]


def draw_coarse_receivers(key, part):
    return build_graph(key)[3]


def block_levels(own_key, dims, cuts, least, largest):
    level = 1.0
    for axis_at, blocks in cuts:
        heights = jax.random.uniform(jax.random.fold_in(jax.random.fold_in(own_key, 6), axis_at), (blocks,), jnp.float32, least / len(cuts), largest / len(cuts))
        level = level * jnp.repeat(jnp.exp(heights), dims[axis_at] // blocks).reshape((-1,) + (1,) * (len(dims) - 1 - axis_at))
    return level


def normal_values(key, dims, scale, bound, shards=(), kind=jnp.bfloat16):
    loudness = block_levels(key, dims, shards, -0.22, 0.18) if shards else 1.0
    result = jax.random.normal(key, dims, jnp.float32) * scale * loudness
    return jnp.minimum(jnp.maximum(result, -bound), bound).astype(kind)


def setup_inputs(seed: int = 0, part: int = 0) -> dict:
    arg_keys = jax.random.split(jax.random.key(seed), 18)
    own_keys = jax.random.split(jax.random.fold_in(arg_keys[17], part), 18)
    node_latent = normal_values(own_keys[0], (NODES, D), 1.0, 6.0, ((0, 16),))
    fine_edges = normal_values(own_keys[1], (FINE_EDGES, D), 1.0, 6.0, ((0, 16),))
    fine_senders = draw_fine_senders(jax.random.fold_in(jax.random.fold_in(arg_keys[17], part), 71), part)
    fine_receivers = draw_fine_receivers(jax.random.fold_in(jax.random.fold_in(arg_keys[17], part), 71), part)
    coarse_edges = normal_values(own_keys[4], (COARSE_EDGES, D), 1.0, 6.0, ((0, 16),))
    coarse_senders = draw_coarse_senders(jax.random.fold_in(jax.random.fold_in(arg_keys[17], part), 71), part)
    coarse_receivers = draw_coarse_receivers(jax.random.fold_in(jax.random.fold_in(arg_keys[17], part), 71), part)
    edge_weight_in = normal_values(arg_keys[7], (3 * D, D), (3 * D) ** -0.5, 0.15625)
    edge_bias = normal_values(arg_keys[8], (D,), 0.5, 3.0, (), jnp.float32)
    edge_weight_out = normal_values(arg_keys[9], (D, D), D ** -0.5, 0.25)
    edge_gain = jnp.clip(1.0 + 0.1 * jax.random.normal(arg_keys[10], (D,), jnp.float32), 0.5, 1.5)
    edge_shift = normal_values(arg_keys[11], (D,), 0.3, 2.0, (), jnp.float32)
    node_weight_in = normal_values(arg_keys[12], (2 * D, D), (2 * D) ** -0.5, 0.1875)
    node_bias = normal_values(arg_keys[13], (D,), 0.5, 3.0, (), jnp.float32)
    node_weight_out = normal_values(arg_keys[14], (D, D), D ** -0.5, 0.25)
    node_gain = jnp.clip(1.0 + 0.1 * jax.random.normal(arg_keys[15], (D,), jnp.float32), 0.5, 1.5)
    node_shift = normal_values(arg_keys[16], (D,), 0.3, 2.0, (), jnp.float32)
    return {"node_latent": node_latent, "fine_edges": fine_edges, "fine_senders": fine_senders, "fine_receivers": fine_receivers, "coarse_edges": coarse_edges, "coarse_senders": coarse_senders, "coarse_receivers": coarse_receivers, "edge_weight_in": edge_weight_in, "edge_bias": edge_bias, "edge_weight_out": edge_weight_out, "edge_gain": edge_gain, "edge_shift": edge_shift, "node_weight_in": node_weight_in, "node_bias": node_bias, "node_weight_out": node_weight_out, "node_gain": node_gain, "node_shift": node_shift}


def layer_norm(values, gain_vector, shift_vector):
    center = values - lax.optimization_barrier(jnp.mean(values, axis=-1, keepdims=True))
    spread = lax.optimization_barrier(jnp.mean(center * center, axis=-1, keepdims=True))
    return center * lax.rsqrt(spread + 1e-05) * gain_vector.astype(jnp.float32) + shift_vector.astype(jnp.float32)

def run_mlp(preact, weight_out, gain_vector, shift_vector):
    hidden = jax.nn.silu(preact).astype(jnp.bfloat16)
    output = jnp.dot(hidden, weight_out, preferred_element_type=jnp.float32)
    return layer_norm(output, gain_vector, shift_vector)

def reference(node_latent, fine_edges, fine_senders, fine_receivers, coarse_edges, coarse_senders, coarse_receivers, edge_weight_in, edge_bias, edge_weight_out, edge_gain, edge_shift, node_weight_in, node_bias, node_weight_out, node_gain, node_shift):
    latent_width = node_latent.shape[1]
    w_edge = edge_weight_in[:latent_width]
    w_send = edge_weight_in[latent_width:2 * latent_width]
    w_recv = edge_weight_in[2 * latent_width:]

    def block_messages(carried):
        edge_block, sender_ids, receiver_ids = carried
        preact = jnp.dot(edge_block, w_edge, preferred_element_type=jnp.float32)
        preact = preact + jnp.dot(node_latent[sender_ids], w_send, preferred_element_type=jnp.float32)
        preact = preact + jnp.dot(node_latent[receiver_ids], w_recv, preferred_element_type=jnp.float32)
        preact = preact + edge_bias.astype(jnp.float32)
        return run_mlp(preact, edge_weight_out, edge_gain, edge_shift).astype(jnp.bfloat16)
    blocks = FINE_EDGES // (FAN * NODE_DEV)
    fine_messages = lax.map(block_messages, (fine_edges.reshape(blocks, -1, latent_width), fine_senders.reshape(blocks, -1), fine_receivers.reshape(blocks, -1)))
    fine_messages = fine_messages.reshape(-1, latent_width)
    coarse_messages = block_messages((coarse_edges, coarse_senders, coarse_receivers))
    summed = jax.ops.segment_sum(fine_messages.astype(jnp.float32), fine_receivers, NODES)
    summed = summed + jax.ops.segment_sum(coarse_messages.astype(jnp.float32), coarse_receivers, NODES)
    summed = summed.astype(jnp.bfloat16)
    node_pre = jnp.dot(node_latent, node_weight_in[:latent_width], preferred_element_type=jnp.float32)
    node_pre = node_pre + jnp.dot(summed, node_weight_in[latent_width:], preferred_element_type=jnp.float32)
    node_pre = node_pre + node_bias.astype(jnp.float32)
    node_update = run_mlp(node_pre, node_weight_out, node_gain, node_shift)
    return (node_latent.astype(jnp.float32) + node_update).astype(jnp.bfloat16)
```

```python
import functools

import jax
import jax.numpy as jnp
from jax import lax
from jax.experimental import pallas as pl
from jax.experimental.pallas import tpu as pltpu
from jax.sharding import PartitionSpec as P

COARSE_DEV = 4
LANES = 128
BF16 = jnp.bfloat16
F32 = jnp.float32


def silu(v):
    u = v * 0.5
    return u + u * jnp.tanh(u)


def layer_norm(values, gain_row, shift_row):
    center = values - jnp.mean(values, axis=-1, keepdims=True)
    spread = jnp.mean(center * center, axis=-1, keepdims=True)
    return center * lax.rsqrt(spread + 1e-05) * gain_row + shift_row


def dot(a, b):
    return jnp.dot(a, b, preferred_element_type=F32)


def columns(row):
    return jnp.broadcast_to(row, (LANES, row.shape[1])).T


def one_hot(cols, width):
    lane = lax.broadcasted_iota(jnp.int32, cols[0].shape, 1)
    blocks = []
    for b in range(width // LANES):
        hit = cols[0] == lane + b * LANES
        for c in cols[1:]:
            hit = hit | (c == lane + b * LANES)
        blocks.append(jnp.where(hit, 1.0, 0.0).astype(BF16))
    return jnp.concatenate(blocks, axis=1)


def local_kernel(
    nodes, halo, n_patches,
    nl, fe, ce, fs, fr, cs, cr, w_in, e_bias, u_in, n_bias,
    base_f, base_c, oh2, sel, inc_f, inc_c, nu, table,
):
    d = nl.shape[1]
    wide = lax.axis_index("wide")
    half = lax.axis_index("narrow")
    device = wide * 2 + half
    x_patch = wide ^ 1
    y_patch = jnp.where(wide % 2 == 0, wide + n_patches - 1, wide + 1) % n_patches
    patch = 2 * nodes
    first = nodes - halo
    block = halo + COARSE_DEV

    node_rows = nl[...]
    table[0:nodes, :] = dot(node_rows, w_in[2 * d : 3 * d, :]).astype(BF16)
    table[nodes : 2 * nodes, :] = dot(node_rows, w_in[d : 2 * d, :]).astype(BF16)
    table[2 * nodes :, :] = jnp.zeros_like(table[2 * nodes :, :])
    nu[...] = dot(node_rows, u_in[0:d, :]) + n_bias[...]

    recv = fr[...] - device * nodes
    send = fs[...]

    def offset(p):
        off = send - p * patch
        inside = (off >= 0) & (off < patch)
        upper = (off >= nodes).astype(jnp.int32)
        return inside, upper, off - upper * nodes

    inside, upper, loc = offset(wide)
    own = jnp.where(inside & (upper == half), loc + nodes, -1)
    pos = jnp.where(inside & (upper != half), loc, -1)
    for k, p in enumerate((x_patch, y_patch)):
        inside, upper, loc = offset(p)
        slot = jnp.where(upper == half, 0, 1)
        at = nodes + k * 2 * block + slot * block + loc - first
        pos = jnp.where(inside, at, pos)

    recv_c = cr[...] - device * nodes
    chip_rows = cs[...].astype(F32)
    owner = jnp.floor((chip_rows + 0.5) * (1.0 / nodes)).astype(jnp.int32)
    slot_c = cs[...] - owner * nodes
    pos_c = ((owner // 2) ^ wide) * (2 * COARSE_DEV) + ((owner % 2) ^ half) * COARSE_DEV + slot_c

    node_at = lax.broadcasted_iota(jnp.int32, (nodes, fr.shape[1]), 0)
    inc_f[...] = jnp.where(node_at == recv, 1.0, 0.0).astype(BF16)
    node_at = lax.broadcasted_iota(jnp.int32, (nodes, cr.shape[1]), 0)
    inc_c[...] = jnp.where(node_at == recv_c, 1.0, 0.0).astype(BF16)

    wide_c = -(-sel.shape[1] // LANES) * LANES
    sel[...] = one_hot((columns(pos_c),), wide_c)[:, : sel.shape[1]]
    oh_c = one_hot((columns(recv_c),), table.shape[0])
    base_c[...] = dot(ce[...], w_in[0:d, :]) + dot(oh_c, table[...]) + e_bias[...]

    recv_cols, own_cols, pos_cols = columns(recv), columns(own), columns(pos)
    oh2[...] = one_hot((pos_cols,), oh2.shape[1])
    rows = fe.shape[0]
    step = rows // 4
    for at in range(0, rows, step):
        s = slice(at, at + step)
        oh1 = one_hot((recv_cols[s], own_cols[s]), table.shape[0])
        base_f[s, :] = dot(fe[s, :], w_in[0:d, :]) + dot(oh1, table[...]) + e_bias[...]


def main_kernel(
    partner, x_rows, y_rows, coarse, nl, base_f, base_c, oh2, sel, inc_f, inc_c, nu,
    w_in, w_out, e_gain, e_shift, u_in, u_out, n_gain, n_shift,
    out, table,
):
    d = nl.shape[1]
    w_send = w_in[d : 2 * d, :]
    a = partner.shape[0]
    b = a + x_rows.shape[0]
    table[0:a, :] = dot(partner[...], w_send).astype(BF16)
    table[a:b, :] = dot(x_rows[...], w_send).astype(BF16)
    table[b:, :] = dot(y_rows[...], w_send).astype(BF16)

    def messages(pre):
        edge_out = dot(silu(pre).astype(BF16), w_out[...])
        return layer_norm(edge_out, e_gain[...], e_shift[...]).astype(BF16)

    picked = dot(sel[...], coarse[...]).astype(BF16)
    summed = dot(inc_c[...], messages(base_c[...] + dot(picked, w_send)))
    rows = base_f.shape[0]
    for at in range(0, rows, 256):
        s = slice(at, min(at + 256, rows))
        pre = base_f[s, :] + dot(oh2[s, :], table[...])
        summed = summed + dot(inc_f[:, s], messages(pre))
    pre = nu[...] + dot(summed.astype(BF16), u_in[d : 2 * d, :])
    update = dot(silu(pre).astype(BF16), u_out[...])
    update = layer_norm(update, n_gain[...], n_shift[...])
    out[...] = (nl[...].astype(F32) + update).astype(BF16)


def vmem(n):
    return [pl.BlockSpec(memory_space=pltpu.VMEM)] * n


def shards(
    node_latent, fine_edges, fine_senders, fine_receivers, coarse_edges, coarse_senders,
    coarse_receivers, edge_weight_in, edge_bias, edge_weight_out, edge_gain, edge_shift,
    node_weight_in, node_bias, node_weight_out, node_gain, node_shift,
):
    nodes, d = node_latent.shape
    halo = nodes // 8
    n_patches = lax.axis_size("wide")
    edges, coarse_count = fine_edges.shape[0], coarse_edges.shape[0]
    row = lambda v: v.reshape(1, -1)

    partner = lax.ppermute(node_latent, "narrow", [(0, 1), (1, 0)])
    pay = jnp.concatenate(
        [node_latent[nodes - halo :], node_latent[:COARSE_DEV], partner[nodes - halo :], partner[:COARSE_DEV]],
        axis=0,
    )
    around = range(n_patches)
    x_rows = lax.ppermute(pay, "wide", [(i, i ^ 1) for i in around])
    y_rows = lax.ppermute(
        pay, "wide", [(i, (i - 1 if i % 2 == 0 else i + 1) % n_patches) for i in around]
    )
    block = halo + COARSE_DEV
    known = jnp.concatenate(
        [pay[halo:block], pay[halo + block :], x_rows[halo:block], x_rows[halo + block :]], axis=0
    )
    have = 2
    while have < n_patches:
        parts = [known]
        for k in range(1, min(4, n_patches // have)):
            parts.append(lax.ppermute(known, "wide", [(i, i ^ (k * have)) for i in around]))
        known = jnp.concatenate(parts, axis=0)
        have *= len(parts)

    table_a = -(-2 * nodes // LANES) * LANES
    table_b = nodes + 4 * block
    shape = jax.ShapeDtypeStruct
    local_out = pl.pallas_call(
        functools.partial(local_kernel, nodes, halo, n_patches),
        out_shape=(
            shape((edges, d), F32),
            shape((coarse_count, d), F32),
            shape((edges, table_b), BF16),
            shape((coarse_count, known.shape[0]), BF16),
            shape((nodes, edges), BF16),
            shape((nodes, coarse_count), BF16),
            shape((nodes, d), F32),
        ),
        in_specs=vmem(11),
        out_specs=tuple(vmem(7)),
        scratch_shapes=[pltpu.VMEM((table_a, d), BF16)],
        name="local",
    )(
        node_latent, fine_edges, coarse_edges, row(fine_senders), row(fine_receivers),
        row(coarse_senders), row(coarse_receivers), edge_weight_in, row(edge_bias),
        node_weight_in, row(node_bias),
    )
    return pl.pallas_call(
        main_kernel,
        out_shape=shape((nodes, d), BF16),
        in_specs=vmem(20),
        out_specs=pl.BlockSpec(memory_space=pltpu.VMEM),
        scratch_shapes=[pltpu.VMEM((table_b, d), BF16)],
        name="main",
    )(
        partner, x_rows, y_rows, known, node_latent, *local_out,
        edge_weight_in, edge_weight_out, row(edge_gain), row(edge_shift),
        node_weight_in, node_weight_out, row(node_gain), row(node_shift),
    )


def solution(mesh):
    axes = ("grp", "wide", "narrow")
    matrix, vector, whole = P(axes, None), P(axes), P()
    return jax.shard_map(
        shards,
        mesh=mesh,
        in_specs=(matrix, matrix, vector, vector, matrix, vector, vector) + (whole,) * 10,
        out_specs=matrix,
        check_vma=False,
    )
```

```python
import functools

import jax
import jax.numpy as jnp
from jax import lax
from jax.experimental import pallas as pl
from jax.experimental.pallas import tpu as pltpu
from jax.sharding import PartitionSpec as P

COARSE_DEV = 4
LANES = 128
TAIL = 16
BF16 = jnp.bfloat16
F32 = jnp.float32
MIB = 1 << 20


def silu(v):
    u = v * 0.5
    return u + u * jnp.tanh(u)


def layer_norm(values, gain_row, shift_row):
    center = values - jnp.mean(values, axis=-1, keepdims=True)
    spread = jnp.mean(center * center, axis=-1, keepdims=True)
    return center * lax.rsqrt(spread + 1e-05) * gain_row + shift_row


def dot(a, b):
    return jnp.dot(a, b, preferred_element_type=F32)


def columns(row):
    return jnp.broadcast_to(row, (LANES, row.shape[1])).T


def one_hot(cols, width):
    lane = lax.broadcasted_iota(jnp.int32, cols[0].shape, 1)
    blocks = []
    for b in range(width // LANES):
        hit = cols[0] == lane + b * LANES
        for c in cols[1:]:
            hit = hit | (c == lane + b * LANES)
        blocks.append(jnp.where(hit, 1.0, 0.0).astype(BF16))
    return jnp.concatenate(blocks, axis=1)


def stage_kernel(*refs):
    n = len(refs) // 2
    sems = refs[2 * n]
    copies = [pltpu.make_async_copy(refs[k], refs[n + k], sems.at[k]) for k in range(n)]
    for c in copies:
        c.start()
    for c in copies:
        c.wait()


def pay_kernel(halo, nl, partner, pay):
    nodes = nl.shape[0]
    pay[...] = jnp.concatenate(
        [nl[nodes - halo :, :], nl[:COARSE_DEV, :], partner[nodes - halo :, :], partner[:COARSE_DEV, :]],
        axis=0,
    )


def pair_kernel(halo, pay, x_rows, known):
    block = halo + COARSE_DEV
    known[...] = jnp.concatenate(
        [r[s : s + COARSE_DEV, :] for r in (pay, x_rows) for s in (halo, block + halo)], axis=0
    )


def join_kernel(*refs):
    at = 0
    for r in refs[:-1]:
        refs[-1][at : at + r.shape[0], :] = r[...]
        at += r.shape[0]


def local_kernel(
    nodes, halo, n_patches,
    nl, fs, fr, cs, cr, e_bias, n_bias, fe_hbm, ce_hbm, w_in, w_out_hbm, u_in, u_out_hbm,
    base_f, base_c, oh2, sel, inc_f, inc_c, nu, w_send, w_out, u_mess, u_out,
    table, fe, ce, w_edge, w_recv, u_node, sems,
):
    d = nl.shape[1]
    rows = fe.shape[0]
    step = rows // 4
    moves = [
        (w_in.at[2 * d : 3 * d, :], w_recv),
        (w_in.at[d : 2 * d, :], w_send),
        (w_in.at[0:d, :], w_edge),
        (ce_hbm, ce),
    ]
    moves += [(fe_hbm.at[k * step : (k + 1) * step, :], fe.at[k * step : (k + 1) * step, :]) for k in range(4)]
    moves += [
        (u_in.at[0:d, :], u_node),
        (w_out_hbm, w_out),
        (u_in.at[d : 2 * d, :], u_mess),
        (u_out_hbm, u_out),
    ]
    copies = [pltpu.make_async_copy(src, dst, sems.at[k]) for k, (src, dst) in enumerate(moves)]
    for c in copies:
        c.start()

    wide = lax.axis_index("wide")
    half = lax.axis_index("narrow")
    device = wide * 2 + half
    x_patch = wide ^ 1
    y_patch = jnp.where(wide % 2 == 0, wide + n_patches - 1, wide + 1) % n_patches
    patch = 2 * nodes
    first = nodes - halo
    block = halo + COARSE_DEV

    recv = fr[...] - device * nodes
    send = fs[...]

    def offset(p):
        off = send - p * patch
        inside = (off >= 0) & (off < patch)
        upper = (off >= nodes).astype(jnp.int32)
        return inside, upper, off - upper * nodes

    inside, upper, loc = offset(wide)
    own = jnp.where(inside & (upper == half), loc + nodes, -1)
    pos = jnp.where(inside & (upper != half), loc, -1)
    for k, p in enumerate((x_patch, y_patch)):
        inside, upper, loc = offset(p)
        slot = jnp.where(upper == half, 0, 1)
        at = nodes + k * 2 * block + slot * block + loc - first
        pos = jnp.where(inside, at, pos)

    recv_c = cr[...] - device * nodes
    chip_rows = cs[...].astype(F32)
    owner = jnp.floor((chip_rows + 0.5) * (1.0 / nodes)).astype(jnp.int32)
    slot_c = cs[...] - owner * nodes
    pos_c = ((owner // 2) ^ wide) * (2 * COARSE_DEV) + ((owner % 2) ^ half) * COARSE_DEV + slot_c

    node_at = lax.broadcasted_iota(jnp.int32, (nodes, fr.shape[1]), 0)
    inc_f[...] = jnp.where(node_at == recv, 1.0, 0.0).astype(BF16)
    node_at = lax.broadcasted_iota(jnp.int32, inc_c.shape, 0)
    inc_c[...] = jnp.where(node_at == recv_c, 1.0, 0.0).astype(BF16)
    wide_c = -(-sel.shape[1] // LANES) * LANES
    sel[...] = one_hot((columns(pos_c),), wide_c)[:, : sel.shape[1]]
    oh_c = one_hot((columns(recv_c),), table.shape[0])
    recv_cols, own_cols, pos_cols = columns(recv), columns(own), columns(pos)
    oh2[...] = one_hot((pos_cols,), oh2.shape[1])
    table[2 * nodes :, :] = jnp.zeros_like(table[2 * nodes :, :])

    node_rows = nl[...]
    copies[0].wait()
    table[0:nodes, :] = dot(node_rows, w_recv[...]).astype(BF16)
    copies[1].wait()
    table[nodes : 2 * nodes, :] = dot(node_rows, w_send[...]).astype(BF16)
    copies[2].wait()
    copies[3].wait()
    base_c[...] = dot(ce[...], w_edge[...]) + dot(oh_c, table[...]) + e_bias[...]
    for k in range(4):
        s = slice(k * step, (k + 1) * step)
        copies[4 + k].wait()
        oh1 = one_hot((recv_cols[s], own_cols[s]), table.shape[0])
        base_f[s, :] = dot(fe[s, :], w_edge[...]) + dot(oh1, table[...]) + e_bias[...]
    copies[8].wait()
    nu[...] = dot(node_rows, u_node[...]) + n_bias[...]
    for c in copies[9:]:
        c.wait()


def messages(pre, w_out, e_gain, e_shift):
    edge_out = dot(silu(pre).astype(BF16), w_out[...])
    return layer_norm(edge_out, e_gain[...], e_shift[...]).astype(BF16)


def node_rows_out(own, pre_own, summed, u_mess, u_out, n_gain, n_shift):
    pre = pre_own + dot(summed.astype(BF16), u_mess[...])
    update = dot(silu(pre).astype(BF16), u_out[...])
    update = layer_norm(update, n_gain[...], n_shift[...])
    return (own.astype(F32) + update).astype(BF16)


def fine_kernel(
    partner, x_rows, y_rows, nl, base_f, oh2, inc_f, nu, w_send, w_out, u_mess, u_out,
    e_gain, e_shift, n_gain, n_shift,
    out, head, table,
):
    a = partner.shape[0]
    b = a + x_rows.shape[0]
    table[0:a, :] = dot(partner[...], w_send[...]).astype(BF16)
    table[a:b, :] = dot(x_rows[...], w_send[...]).astype(BF16)
    table[b:, :] = dot(y_rows[...], w_send[...]).astype(BF16)
    rows = base_f.shape[0]
    summed = jnp.zeros(nl.shape, F32)
    for at in range(0, rows, 256):
        s = slice(at, min(at + 256, rows))
        pre = base_f[s, :] + dot(oh2[s, :], table[...])
        summed = summed + dot(inc_f[:, s], messages(pre, w_out, e_gain, e_shift))
    head[...] = summed[:TAIL, :]
    out[...] = node_rows_out(nl[...], nu[...], summed, u_mess, u_out, n_gain, n_shift)


def coarse_kernel(
    n_pieces, out_f, head, nl, nu, base_c, sel, inc_c, w_send, w_out, u_mess, u_out,
    e_gain, e_shift, n_gain, n_shift, *rest,
):
    pieces, (out, rows) = rest[:n_pieces], rest[n_pieces:]
    at = 0
    for r in pieces:
        rows[at : at + r.shape[0], :] = r[...]
        at += r.shape[0]
    picked = dot(sel[...], rows[...]).astype(BF16)
    pre = base_c[...] + dot(picked, w_send[...])
    summed = head[...] + dot(inc_c[...], messages(pre, w_out, e_gain, e_shift))
    out[TAIL:, :] = out_f[TAIL:, :]
    out[:TAIL, :] = node_rows_out(nl[:TAIL, :], nu[:TAIL, :], summed, u_mess, u_out, n_gain, n_shift)


NEAR = pl.BlockSpec(memory_space=pltpu.VMEM)
FAR = pl.BlockSpec(memory_space=pltpu.HBM)


def near(*arrays):
    return [pltpu.with_memory_space_constraint(a, pltpu.VMEM) for a in arrays]


def call(kernel, near_in, outs, name, far_in=(), scratch=(), limit=8, far_out=False, cost=None):
    outs = [(o.shape, o.dtype) if hasattr(o, "shape") else o for o in outs]
    kind = (lambda s, t: jax.ShapeDtypeStruct(s, t)) if far_out else (lambda s, t: pltpu.VMEM(s, t))
    return pl.pallas_call(
        kernel,
        out_shape=tuple(kind(*o) for o in outs),
        in_specs=[NEAR] * len(near_in) + [FAR] * len(far_in),
        out_specs=tuple([NEAR] * len(outs)),
        scratch_shapes=list(scratch),
        compiler_params=pltpu.CompilerParams(vmem_limit_bytes=limit * MIB),
        cost_estimate=pl.CostEstimate(flops=cost or 0, bytes_accessed=cost or 0, transcendentals=0),
        name=name,
    )(*near(*near_in), *[pltpu.with_memory_space_constraint(a, pltpu.HBM) for a in far_in])


def shards(
    node_latent, fine_edges, fine_senders, fine_receivers, coarse_edges, coarse_senders,
    coarse_receivers, edge_weight_in, edge_bias, edge_weight_out, edge_gain, edge_shift,
    node_weight_in, node_bias, node_weight_out, node_gain, node_shift,
):
    nodes, d = node_latent.shape
    halo = nodes // 8
    block = halo + COARSE_DEV
    n_patches = lax.axis_size("wide")
    edges, coarse_count = fine_edges.shape[0], coarse_edges.shape[0]
    small = [node_latent] + [
        v.reshape(1, -1)
        for v in (
            fine_senders, fine_receivers, coarse_senders, coarse_receivers, edge_bias, node_bias,
            edge_gain, edge_shift, node_gain, node_shift,
        )
    ]
    dma = pltpu.SemaphoreType.DMA

    partner = lax.ppermute(node_latent, "narrow", [(0, 1), (1, 0)])
    nl, fs, fr, cs, cr, e_bias, n_bias, e_gain, e_shift, n_gain, n_shift = call(
        stage_kernel, (), small, "stage", far_in=small, scratch=[dma((len(small),))], limit=1
    )
    (pay,) = call(functools.partial(pay_kernel, halo), (nl, partner), [((2 * block, d), BF16)], "pay", limit=1)
    around = range(n_patches)
    x_rows = lax.ppermute(pay, "wide", [(i, i ^ 1) for i in around])
    y_rows = lax.ppermute(
        pay, "wide", [(i, (i - 1 if i % 2 == 0 else i + 1) % n_patches) for i in around]
    )
    (known,) = call(
        functools.partial(pair_kernel, halo), (pay, x_rows), [((4 * COARSE_DEV, d), BF16)], "pair", limit=1
    )
    have = 2
    while True:
        pieces = [known]
        for k in range(1, min(4, n_patches // have)):
            pieces.append(lax.ppermute(known, "wide", [(i, i ^ (k * have)) for i in around]))
        have *= len(pieces)
        if have == n_patches:
            break
        (known,) = call(
            join_kernel, pieces, [((len(pieces) * known.shape[0], d), BF16)], "join", limit=2
        )
    coarse_rows = len(pieces) * known.shape[0]

    table_a = -(-2 * nodes // LANES) * LANES
    table_b = nodes + 4 * block
    square = ((d, d), BF16)
    base_f, base_c, oh2, sel, inc_f, inc_c, nu, w_send, w_out, u_mess, u_out = call(
        functools.partial(local_kernel, nodes, halo, n_patches),
        (nl, fs, fr, cs, cr, e_bias, n_bias),
        [
            ((edges, d), F32),
            ((coarse_count, d), F32),
            ((edges, table_b), BF16),
            ((coarse_count, coarse_rows), BF16),
            ((nodes, edges), BF16),
            ((TAIL, coarse_count), BF16),
            ((nodes, d), F32),
            square, square, square, square,
        ],
        "local",
        far_in=(fine_edges, coarse_edges, edge_weight_in, edge_weight_out, node_weight_in, node_weight_out),
        scratch=[
            pltpu.VMEM((table_a, d), BF16),
            pltpu.VMEM((edges, d), BF16),
            pltpu.VMEM((coarse_count, d), BF16),
            pltpu.VMEM((d, d), BF16),
            pltpu.VMEM((d, d), BF16),
            pltpu.VMEM((d, d), BF16),
            dma((12,)),
        ],
        limit=16,
    )
    out_f, head = call(
        fine_kernel,
        (partner, x_rows, y_rows, nl, base_f, oh2, inc_f, nu, w_send, w_out, u_mess, u_out,
         e_gain, e_shift, n_gain, n_shift),
        [((nodes, d), BF16), ((TAIL, d), F32)],
        "fine",
        scratch=[pltpu.VMEM((table_b, d), BF16)],
        limit=16,
    )
    (out,) = call(
        functools.partial(coarse_kernel, len(pieces)),
        (out_f, head, nl, nu, base_c, sel, inc_c, w_send, w_out, u_mess, u_out,
         e_gain, e_shift, n_gain, n_shift, *pieces),
        [((nodes, d), BF16)],
        "coarse",
        scratch=[pltpu.VMEM((coarse_rows, d), BF16)],
        limit=8,
        far_out=True,
    )
    return out


def solution(mesh):
    axes = ("grp", "wide", "narrow")
    matrix, vector, whole = P(axes, None), P(axes), P()
    return jax.shard_map(
        shards,
        mesh=mesh,
        in_specs=(matrix, matrix, vector, vector, matrix, vector, vector) + (whole,) * 10,
        out_specs=matrix,
        check_vma=False,
    )
```

```python
import functools

import jax
import jax.numpy as jnp
from jax import lax
from jax.experimental import pallas as pl
from jax.experimental.pallas import tpu as pltpu
from jax.sharding import PartitionSpec as P


COARSE_DEV = 4
LANES = 128
CHUNKS = 3
BF16 = jnp.bfloat16
F32 = jnp.float32
MIB = 1 << 20


def silu_of_half(u):
    return u + u * jnp.tanh(u)


def normalized(values):
    center = values - jnp.mean(values, axis=-1, keepdims=True)
    spread = jnp.mean(center * center, axis=-1, keepdims=True)
    return center * lax.rsqrt(spread + 1e-05)


def dot(a, b):
    return jnp.dot(a, b, preferred_element_type=F32)


def columns(row):
    return jnp.broadcast_to(row, (LANES, row.shape[1])).T


def one_hot(cols, width, value=1.0):
    lane = lax.broadcasted_iota(jnp.int32, cols[0].shape, 1)
    blocks = []
    for b in range(width // LANES):
        hit = cols[0] == lane + b * LANES
        for c in cols[1:]:
            hit = hit | (c == lane + b * LANES)
        blocks.append(jnp.where(hit, value, 0.0).astype(BF16))
    return jnp.concatenate(blocks, axis=1)


def stage_kernel(n, *refs):
    sems = refs[-1]
    copies = [pltpu.make_async_copy(refs[k], refs[k - n - 1], sems.at[k]) for k in range(n)]
    for c in copies:
        c.start()
    for c in copies:
        c.wait()


def pay_kernel(halo, nl, partner, pay):
    nodes = nl.shape[0]
    pay[...] = jnp.concatenate(
        [nl[nodes - halo :, :], nl[:COARSE_DEV, :], partner[nodes - halo :, :], partner[:COARSE_DEV, :]],
        axis=0,
    )


def pair_kernel(halo, pay, x_rows, _, known, rich):
    block = halo + COARSE_DEV
    pair = jnp.concatenate(
        [r[s : s + COARSE_DEV, :] for r in (pay, x_rows) for s in (halo, block + halo)], axis=0
    )
    known[...] = pair
    rich[: pair.shape[0], :] = pair
    rich[pair.shape[0] :, :] = x_rows[...]


def join_kernel(*refs):
    at = 0
    for r in refs[:-1]:
        refs[-1][at : at + r.shape[0], :] = r[...]
        at += r.shape[0]


def places(n_patches):
    wide = lax.axis_index("wide")
    half = lax.axis_index("narrow")
    y_patch = jnp.where(wide % 2 == 0, wide + n_patches - 1, wide + 1) % n_patches
    return wide, half, wide * 2 + half, y_patch


def local_kernel(
    nodes, halo, n_patches,
    nl, fs, fr, cs, cr, e_bias, n_bias, e_shift, ce, w_in, u_in,
    base_c, oh1, oh2, sel, inc, shifts, nu, table,
):
    d = nl.shape[1]
    wide, half, device, y_patch = places(n_patches)
    patch = 2 * nodes
    first = nodes - halo
    block = halo + COARSE_DEV

    recv = fr[...] - device * nodes
    send = fs[...]

    def offset(p):
        off = send - p * patch
        inside = (off >= 0) & (off < patch)
        upper = (off >= nodes).astype(jnp.int32)
        return inside, upper, off - upper * nodes

    inside, upper, loc = offset(wide)
    own = jnp.where(inside & (upper == half), loc + nodes, -1)
    pos = jnp.where(inside & (upper != half), loc, -1)
    for k, p in enumerate((wide ^ 1, y_patch)):
        inside, upper, loc = offset(p)
        slot = jnp.where(upper == half, 0, 1)
        at = nodes + k * 2 * block + slot * block + loc - first
        pos = jnp.where(inside, at, pos)

    recv_c = cr[...] - device * nodes
    chip_rows = cs[...].astype(F32)
    owner = jnp.floor((chip_rows + 0.5) * (1.0 / nodes)).astype(jnp.int32)
    slot_c = cs[...] - owner * nodes
    pos_c = ((owner // 2) ^ wide) * (2 * COARSE_DEV) + ((owner % 2) ^ half) * COARSE_DEV + slot_c

    total = fr.shape[1] + cr.shape[1]
    spare = jnp.full((1, inc.shape[1] - total), -1, jnp.int32)
    recv_all = jnp.concatenate([recv, recv_c, spare], axis=1)
    node_at = lax.broadcasted_iota(jnp.int32, inc.shape, 0)
    marks = jnp.where(node_at == recv_all, 1.0, 0.0)
    inc[...] = marks.astype(BF16)
    shifts[...] = jnp.sum(marks, axis=1, keepdims=True) * e_shift[...]
    wide_c = -(-sel.shape[1] // LANES) * LANES
    sel[...] = one_hot((columns(pos_c),), wide_c)[:, : sel.shape[1]]
    oh_c = one_hot((columns(recv_c),), table.shape[0])
    oh1[...] = one_hot((columns(recv), columns(own)), oh1.shape[1], 0.5)
    oh2[...] = one_hot((columns(pos),), oh2.shape[1], 0.5)
    table[2 * nodes :, :] = jnp.zeros_like(table[2 * nodes :, :])

    node_rows = nl[...]
    table[0:nodes, :] = dot(node_rows, w_in[2 * d :, :]).astype(BF16)
    table[nodes : 2 * nodes, :] = dot(node_rows, w_in[d : 2 * d, :]).astype(BF16)
    nu[...] = 0.5 * (dot(node_rows, u_in[:d, :]) + n_bias[...])
    base_c[...] = 0.5 * (dot(ce[...], w_in[:d, :]) + dot(oh_c, table[...]) + e_bias[...])


def base_kernel(oh1, table, w_in, e_bias, fe, base_f):
    rows, d = fe.shape
    step = rows // 2
    for k in range(2):
        s = slice(k * step, (k + 1) * step)
        own = 0.5 * (dot(fe[s, :], w_in[:d, :]) + e_bias[...])
        base_f[s, :] = own + dot(oh1[s, :], table[...])


def w_send(w_in):
    d = w_in.shape[1]
    return w_in[d : 2 * d, :]


def main_kernel(
    n_patches, y_choices, n_pieces,
    partner, x_rows, nl, base_f, base_c, oh2, sel, inc, shifts, nu, w_in, w_out, u_in, u_out,
    e_gain, n_gain, n_shift, *refs,
):
    y_refs, refs = refs[: len(y_choices)], refs[len(y_choices) :]
    pieces, (out, table, picks, hidden, mess) = refs[:n_pieces], refs[n_pieces:]
    a = partner.shape[0]
    b = a + x_rows.shape[0]
    n_rows = x_rows.shape[0]
    y_rows = y_refs[0][y_refs[0].shape[0] - n_rows :, :]
    if len(y_choices) > 1:
        wide, _, _, y_patch = places(n_patches)
        pair_step = (wide // 2) ^ (y_patch // 2)
        for k, ref in zip(y_choices[1:], y_refs[1:]):
            y_rows = jnp.where(pair_step == k, ref[ref.shape[0] - n_rows :, :], y_rows)
    size = picks.shape[0] // n_pieces
    for k, r in enumerate(pieces):
        picks[k * size : (k + 1) * size, :] = r[:size, :]
    table[0:a, :] = partner[...]
    table[a:b, :] = x_rows[...]
    table[b:, :] = y_rows
    w_s = w_send(w_in)
    table[...] = dot(table[...], w_s).astype(BF16)

    rows, coarse = base_f.shape[0], base_c.shape[0]
    step = rows // CHUNKS
    parts = [slice(k * step, (k + 1) * step) for k in range(CHUNKS)] + [slice(rows, rows + coarse)]

    def first(k):
        s = parts[k]
        if k < CHUNKS:
            half = base_f[s, :] + dot(oh2[s, :], table[...])
        else:
            picked = dot(sel[...], picks[...]).astype(BF16)
            half = base_c[...] + 0.5 * dot(picked, w_s)
        hidden[s, :] = silu_of_half(half).astype(BF16)

    def second(k):
        s = parts[k]
        mess[s, :] = normalized(dot(hidden[s, :], w_out[...])).astype(BF16)

    mess[rows + coarse :, :] = jnp.zeros_like(mess[rows + coarse :, :])
    order = [CHUNKS] + list(range(CHUNKS))
    first(order[0])
    for now, then in zip(order, order[1:]):
        first(then)
        second(now)
    second(order[-1])
    summed = dot(inc[...], mess[...]) * e_gain[...] + shifts[...]
    d = nl.shape[1]
    half = nu[...] + 0.5 * dot(summed.astype(BF16), u_in[d:, :])
    update = normalized(dot(silu_of_half(half).astype(BF16), u_out[...]))
    out[...] = (nl[...].astype(F32) + (update * n_gain[...] + n_shift[...])).astype(BF16)


NEAR = pl.BlockSpec(memory_space=pltpu.VMEM)
FAR = pl.BlockSpec(memory_space=pltpu.HBM)


def near(*arrays):
    return [pltpu.with_memory_space_constraint(a, pltpu.VMEM) for a in arrays]


def call(kernel, near_in, outs, far_in=(), scratch=(), limit=8, far_out=False, cost=None):
    outs = [(o.shape, o.dtype) if hasattr(o, "shape") else o for o in outs]
    kind = (lambda s, t: jax.ShapeDtypeStruct(s, t)) if far_out else (lambda s, t: pltpu.VMEM(s, t))
    return pl.pallas_call(
        kernel,
        out_shape=tuple(kind(*o) for o in outs),
        in_specs=[NEAR] * len(near_in) + [FAR] * len(far_in),
        out_specs=tuple([NEAR] * len(outs)),
        scratch_shapes=list(scratch),
        compiler_params=pltpu.CompilerParams(vmem_limit_bytes=limit * MIB),
        cost_estimate=pl.CostEstimate(flops=cost or 0, bytes_accessed=cost or 0, transcendentals=0),
    )(*near(*near_in), *[pltpu.with_memory_space_constraint(a, pltpu.HBM) for a in far_in])


def shards(
    node_latent, fine_edges, fine_senders, fine_receivers, coarse_edges, coarse_senders,
    coarse_receivers, edge_weight_in, edge_bias, edge_weight_out, edge_gain, edge_shift,
    node_weight_in, node_bias, node_weight_out, node_gain, node_shift,
):
    nodes, d = node_latent.shape
    halo = nodes // 8
    block = halo + COARSE_DEV
    n_patches = lax.axis_size("wide")
    edges, coarse_count = fine_edges.shape[0], coarse_edges.shape[0]
    small = [node_latent] + [
        v.reshape(1, -1)
        for v in (
            fine_senders, fine_receivers, coarse_senders, coarse_receivers, edge_bias, node_bias,
            edge_gain, edge_shift, node_gain, node_shift,
        )
    ]
    dma = pltpu.SemaphoreType.DMA

    partner = lax.ppermute(node_latent, "narrow", [(0, 1), (1, 0)])
    nl, fs, fr, cs, cr, e_bias, n_bias, e_gain, e_shift, n_gain, n_shift = call(
        functools.partial(stage_kernel, len(small)), (), small,
        far_in=small + [fine_edges, edge_weight_in, node_weight_in], scratch=[dma((len(small),))], limit=1
    )
    (pay,) = call(functools.partial(pay_kernel, halo), (nl, partner), [((2 * block, d), BF16)], limit=1)
    around = range(n_patches)
    x_rows = lax.ppermute(pay, "wide", [(i, i ^ 1) for i in around])
    table_a = -(-2 * nodes // LANES) * LANES
    table_b = nodes + 4 * block
    padded = -(-(edges + coarse_count) // LANES) * LANES
    base_c, oh1, oh2, sel, inc, shifts, nu, table = call(
        functools.partial(local_kernel, nodes, halo, n_patches),
        (nl, fs, fr, cs, cr, e_bias, n_bias, e_shift, coarse_edges, edge_weight_in, node_weight_in),
        [
            ((coarse_count, d), F32),
            ((edges, table_a), BF16),
            ((edges, table_b), BF16),
            ((coarse_count, 2 * n_patches * COARSE_DEV), BF16),
            ((nodes, padded), BF16),
            ((nodes, d), F32),
            ((nodes, d), F32),
            ((table_a, d), BF16),
        ],
        limit=16,
    )
    known, rich = call(
        functools.partial(pair_kernel, halo), (pay, x_rows, base_c),
        [((4 * COARSE_DEV, d), BF16), ((4 * COARSE_DEV + 2 * block, d), BF16)], limit=1,
    )
    shift = lambda v, k: lax.ppermute(v, "wide", [(i, i ^ k) for i in around])
    near_ring = n_patches == 8
    if near_ring:
        three = shift(rich, 6)
        two = shift(known, 4)
        one = shift(rich, 2)
        pieces = [known, one, two, three]
        y_choices, y_refs = (1, 3), (one, three)
    else:
        y_choices = (0,)
        y_refs = (
            lax.ppermute(
                pay, "wide", [(i, (i - 1 if i % 2 == 0 else i + 1) % n_patches) for i in around]
            ),
        )
        have = 2
        while True:
            pieces = [known]
            for k in range(1, min(4, n_patches // have)):
                pieces.append(shift(known, k * have))
            have *= len(pieces)
            if have == n_patches:
                break
            (known,) = call(
                join_kernel, pieces, [((len(pieces) * known.shape[0], d), BF16)], limit=2
            )
    coarse_rows = len(pieces) * known.shape[0]

    (base_f,) = call(
        base_kernel, (oh1, table, edge_weight_in, e_bias, fine_edges), [((edges, d), F32)], limit=16
    )
    (out,) = call(
        functools.partial(main_kernel, n_patches, y_choices, len(pieces)),
        (partner, x_rows, nl, base_f, base_c, oh2, sel, inc, shifts, nu,
         edge_weight_in, edge_weight_out, node_weight_in, node_weight_out,
         e_gain, n_gain, n_shift, *y_refs, *pieces),
        [((nodes, d), BF16)],
        scratch=[
            pltpu.VMEM((table_b, d), BF16),
            pltpu.VMEM((coarse_rows, d), BF16),
            pltpu.VMEM((padded, d), BF16),
            pltpu.VMEM((padded, d), BF16),
        ],
        limit=16,
        far_out=True,
    )
    return out


def solution(mesh):
    axes = ("grp", "wide", "narrow")
    matrix, vector, whole = P(axes, None), P(axes), P()
    return jax.shard_map(
        shards,
        mesh=mesh,
        in_specs=(matrix, matrix, vector, vector, matrix, vector, vector) + (whole,) * 10,
        out_specs=matrix,
        check_vma=False,
    )
```

```python
import functools

import jax
import jax.numpy as jnp
from jax import lax
from jax.experimental import pallas as pl
from jax.experimental.pallas import tpu as pltpu
from jax.sharding import PartitionSpec as P


COARSE_DEV = 4
LANES = 128
CHUNKS = 3
RING = 8
BF16 = jnp.bfloat16
F32 = jnp.float32
MIB = 1 << 20


def silu_of_half(u):
    return u + u * jnp.tanh(u)


def normalized(values):
    center = values - jnp.mean(values, axis=-1, keepdims=True)
    spread = jnp.mean(center * center, axis=-1, keepdims=True)
    return center * lax.rsqrt(spread + 1e-05)


def dot(a, b):
    return jnp.dot(a, b, preferred_element_type=F32)


def columns(row):
    return jnp.broadcast_to(row, (LANES, row.shape[1])).T


def one_hot(cols, width, value=1.0):
    lane = lax.broadcasted_iota(jnp.int32, cols[0].shape, 1)
    blocks = []
    for b in range(width // LANES):
        hit = cols[0] == lane + b * LANES
        for c in cols[1:]:
            hit = hit | (c == lane + b * LANES)
        blocks.append(jnp.where(hit, value, 0.0).astype(BF16))
    return jnp.concatenate(blocks, axis=1)


def stage_kernel(n, *refs):
    sems = refs[-1]
    copies = [pltpu.make_async_copy(refs[k], refs[k - n - 1], sems.at[k]) for k in range(n)]
    for c in copies:
        c.start()
    for c in copies:
        c.wait()


def pay_kernel(halo, nl, partner, pay):
    nodes = nl.shape[0]
    pick = lambda r: jnp.concatenate([r[nodes - halo :, :], r[:COARSE_DEV, :]], axis=0)
    own, other = pick(nl), pick(partner)
    low = lax.axis_index("narrow") == 0
    pay[...] = jnp.concatenate([jnp.where(low, own, other), jnp.where(low, other, own)], axis=0)


def coarse_of(rows, halo):
    block = halo + COARSE_DEV
    return [rows[halo:block, :], rows[block + halo : 2 * block, :]]


def pair_kernel(halo, pay, x_rows, _, known, rich):
    known[...] = jnp.concatenate(coarse_of(pay, halo) + coarse_of(x_rows, halo), axis=0)
    rich[...] = jnp.concatenate([known[...]] + halos_of(x_rows, halo), axis=0)


def both_kernel(first, second, _, both):
    low = lax.axis_index("narrow") == 0
    n, m = first.shape[0], both.shape[0] - first.shape[0]
    both[:n, :] = jnp.where(low, first[...], second[...])
    both[n:, :] = first[:m, :]


def halos_of(rows, halo):
    block = halo + COARSE_DEV
    return [rows[:halo, :], rows[block : block + halo, :]]


def collect_kernel(halo, x_rows, known, both, other, far, picks):
    n, m = 2 * halo, known.shape[0]
    low = lax.axis_index("narrow") == 0
    even = lax.axis_index("wide") % 2 == 0
    zero, one = jnp.where(low, both[...], other[...]), jnp.where(low, other[...], both[...])
    picks[...] = jnp.concatenate([known[...], one[:m], one[m + n :], zero[:m]], axis=0)
    source = jnp.where(even, zero[m : m + n], one[m : m + n])
    far[...] = jnp.concatenate([x_rows[...], source, known[: 2 * COARSE_DEV]], axis=0)


def wrap_kernel(halo, x_rows, y_rows, far):
    far[...] = jnp.concatenate(
        [x_rows[...]] + halos_of(y_rows[...], halo) + [y_rows[: 2 * COARSE_DEV, :]], axis=0
    )


def join_kernel(*refs):
    at = 0
    for r in refs[:-1]:
        refs[-1][at : at + r.shape[0], :] = r[...]
        at += r.shape[0]


def places(n_patches):
    wide = lax.axis_index("wide")
    half = lax.axis_index("narrow")
    y_patch = jnp.where(wide % 2 == 0, wide + n_patches - 1, wide + 1) % n_patches
    return wide, half, wide * 2 + half, y_patch


def local_kernel(
    nodes, halo, n_patches,
    nl, fs, fr, cs, cr, e_bias, n_bias, e_shift, ce, w_in, u_in,
    base_c, oh1, oh2, sel, inc, shifts, nu, table,
):
    d = nl.shape[1]
    wide, half, device, y_patch = places(n_patches)
    patch = 2 * nodes
    first = nodes - halo
    block = halo + COARSE_DEV

    recv = fr[...] - device * nodes
    send = fs[...]

    def offset(p):
        off = send - p * patch
        inside = (off >= 0) & (off < patch)
        upper = (off >= nodes).astype(jnp.int32)
        return inside, upper, off - upper * nodes

    inside, upper, loc = offset(wide)
    own = jnp.where(inside & (upper == half), loc + nodes, -1)
    pos = jnp.where(inside & (upper != half), loc, -1)
    for k, p in enumerate((wide ^ 1, y_patch)):
        inside, upper, loc = offset(p)
        at = nodes + k * 2 * block + upper * (block, halo)[k] + loc - first
        pos = jnp.where(inside, at, pos)

    recv_c = cr[...] - device * nodes
    chip_rows = cs[...].astype(F32)
    owner = jnp.floor((chip_rows + 0.5) * (1.0 / nodes)).astype(jnp.int32)
    slot_c = cs[...] - owner * nodes
    patch_c = owner // 2
    if n_patches == RING:
        pairs = n_patches // 2
        place_c = (patch_c // 2 - wide // 2 + pairs) % pairs * 2 + (patch_c ^ wide) % 2
    else:
        place_c = patch_c ^ wide
    pos_c = place_c * (2 * COARSE_DEV) + (owner % 2) * COARSE_DEV + slot_c
    total = fr.shape[1] + cr.shape[1]
    spare = jnp.full((1, inc.shape[1] - total), -1, jnp.int32)
    recv_all = jnp.concatenate([recv, recv_c, spare], axis=1)
    node_at = lax.broadcasted_iota(jnp.int32, inc.shape, 0)
    marks = jnp.where(node_at == recv_all, 1.0, 0.0)
    inc[...] = marks.astype(BF16)
    shifts[...] = jnp.sum(marks, axis=1, keepdims=True) * e_shift[...]
    wide_c = -(-sel.shape[1] // LANES) * LANES
    sel[...] = one_hot((columns(pos_c),), wide_c)[:, : sel.shape[1]]
    oh_c = one_hot((columns(recv_c),), table.shape[0])
    oh1[...] = one_hot((columns(recv), columns(own)), oh1.shape[1], 0.5)
    oh2[...] = one_hot((columns(pos),), oh2.shape[1], 0.5)
    table[2 * nodes :, :] = jnp.zeros_like(table[2 * nodes :, :])

    node_rows = nl[...]
    table[0:nodes, :] = dot(node_rows, w_in[2 * d :, :]).astype(BF16)
    table[nodes : 2 * nodes, :] = dot(node_rows, w_in[d : 2 * d, :]).astype(BF16)
    nu[...] = 0.5 * (dot(node_rows, u_in[:d, :]) + n_bias[...])
    base_c[...] = 0.5 * (dot(ce[...], w_in[:d, :]) + dot(oh_c, table[...]) + e_bias[...])


def base_kernel(oh1, table, w_in, e_bias, fe, base_f):
    rows, d = fe.shape
    step = rows // 2
    for k in range(2):
        s = slice(k * step, (k + 1) * step)
        own = 0.5 * (dot(fe[s, :], w_in[:d, :]) + e_bias[...])
        base_f[s, :] = own + dot(oh1[s, :], table[...])


def w_send(w_in):
    d = w_in.shape[1]
    return w_in[d : 2 * d, :]


def main_kernel(
    partner, far, nl, base_f, base_c, oh2, sel, inc, shifts, nu, w_in, w_out, u_in, u_out,
    e_gain, n_gain, n_shift, *refs,
):
    pieces, (out, table, picks, hidden, mess) = refs[:-5], refs[-5:]
    picks[...] = jnp.concatenate([r[...] for r in pieces], axis=0)
    a = partner.shape[0]
    table[0:a, :] = partner[...]
    table[a:, :] = far[...]
    w_s = w_send(w_in)
    table[...] = dot(table[...], w_s).astype(BF16)

    rows, coarse = base_f.shape[0], base_c.shape[0]
    step = rows // CHUNKS
    parts = [slice(k * step, (k + 1) * step) for k in range(CHUNKS)] + [slice(rows, rows + coarse)]

    def first(k):
        s = parts[k]
        if k < CHUNKS:
            half = base_f[s, :] + dot(oh2[s, :], table[...])
        else:
            picked = dot(sel[...], picks[...]).astype(BF16)
            half = base_c[...] + 0.5 * dot(picked, w_s)
        hidden[s, :] = silu_of_half(half).astype(BF16)

    def second(k):
        s = parts[k]
        mess[s, :] = normalized(dot(hidden[s, :], w_out[...])).astype(BF16)

    mess[rows + coarse :, :] = jnp.zeros_like(mess[rows + coarse :, :])
    order = [CHUNKS] + list(range(CHUNKS))
    first(order[0])
    for now, then in zip(order, order[1:]):
        first(then)
        second(now)
    second(order[-1])
    summed = dot(inc[...], mess[...]) * e_gain[...] + shifts[...]
    d = nl.shape[1]
    half = nu[...] + 0.5 * dot(summed.astype(BF16), u_in[d:, :])
    update = normalized(dot(silu_of_half(half).astype(BF16), u_out[...]))
    out[...] = (nl[...].astype(F32) + (update * n_gain[...] + n_shift[...])).astype(BF16)


NEAR = pl.BlockSpec(memory_space=pltpu.VMEM)
FAR = pl.BlockSpec(memory_space=pltpu.HBM)


def near(*arrays):
    return [pltpu.with_memory_space_constraint(a, pltpu.VMEM) for a in arrays]


def call(kernel, near_in, outs, far_in=(), scratch=(), limit=8, far_out=False, cost=None):
    outs = [(o.shape, o.dtype) if hasattr(o, "shape") else o for o in outs]
    kind = (lambda s, t: jax.ShapeDtypeStruct(s, t)) if far_out else (lambda s, t: pltpu.VMEM(s, t))
    return pl.pallas_call(
        kernel,
        out_shape=tuple(kind(*o) for o in outs),
        in_specs=[NEAR] * len(near_in) + [FAR] * len(far_in),
        out_specs=tuple([NEAR] * len(outs)),
        scratch_shapes=list(scratch),
        compiler_params=pltpu.CompilerParams(vmem_limit_bytes=limit * MIB),
        cost_estimate=pl.CostEstimate(flops=cost or 0, bytes_accessed=cost or 0, transcendentals=0),
    )(*near(*near_in), *[pltpu.with_memory_space_constraint(a, pltpu.HBM) for a in far_in])


def shards(
    node_latent, fine_edges, fine_senders, fine_receivers, coarse_edges, coarse_senders,
    coarse_receivers, edge_weight_in, edge_bias, edge_weight_out, edge_gain, edge_shift,
    node_weight_in, node_bias, node_weight_out, node_gain, node_shift,
):
    nodes, d = node_latent.shape
    halo = nodes // 8
    block = halo + COARSE_DEV
    n_patches = lax.axis_size("wide")
    edges, coarse_count = fine_edges.shape[0], coarse_edges.shape[0]
    small = [node_latent] + [
        v.reshape(1, -1)
        for v in (
            fine_senders, fine_receivers, coarse_senders, coarse_receivers, edge_bias, node_bias,
            edge_gain, edge_shift, node_gain, node_shift,
        )
    ]
    dma = pltpu.SemaphoreType.DMA

    partner = lax.ppermute(node_latent, "narrow", [(0, 1), (1, 0)])
    nl, fs, fr, cs, cr, e_bias, n_bias, e_gain, e_shift, n_gain, n_shift = call(
        functools.partial(stage_kernel, len(small)), (), small,
        far_in=small + [fine_edges, edge_weight_in, node_weight_in], scratch=[dma((len(small),))], limit=1
    )
    (pay,) = call(functools.partial(pay_kernel, halo), (nl, partner), [((2 * block, d), BF16)], limit=1)
    around = range(n_patches)
    table_a = -(-2 * nodes // LANES) * LANES
    table_b = nodes + 4 * block
    padded = -(-(edges + coarse_count) // LANES) * LANES
    base_c, oh1, oh2, sel, inc, shifts, nu, table = call(
        functools.partial(local_kernel, nodes, halo, n_patches),
        (nl, fs, fr, cs, cr, e_bias, n_bias, e_shift, coarse_edges, edge_weight_in, node_weight_in),
        [
            ((coarse_count, d), F32),
            ((edges, table_a), BF16),
            ((edges, table_b), BF16),
            ((coarse_count, 2 * n_patches * COARSE_DEV), BF16),
            ((nodes, padded), BF16),
            ((nodes, d), F32),
            ((nodes, d), F32),
            ((table_a, d), BF16),
        ],
        limit=16,
    )
    shift = lambda v, k: lax.ppermute(v, "wide", [(i, i ^ k) for i in around])
    x_rows = shift(pay, 1)
    known, rich = call(
        functools.partial(pair_kernel, halo), (pay, x_rows, base_c),
        [((4 * COARSE_DEV, d), BF16), ((4 * COARSE_DEV + 2 * halo, d), BF16)], limit=1,
    )
    if n_patches == RING:
        spot = lambda p, c: p % n_patches * 2 + c
        split = lambda v, steps: lax.ppermute(
            v, ("wide", "narrow"),
            [(spot(p, c), spot(steps[c](p), c)) for p in around for c in range(2)],
        )
        first = split(rich, (lambda p: p + 2, lambda p: p + 4))
        second = split(rich, (lambda p: p ^ 1, lambda p: p - 2))
        (both,) = call(
            both_kernel, (first, second, base_c), [((8 * COARSE_DEV + 2 * halo, d), BF16)], limit=1
        )
        other = lax.ppermute(both, "narrow", [(0, 1), (1, 0)])
        far, picks = call(
            functools.partial(collect_kernel, halo), (x_rows, known, both, other),
            [((4 * block, d), BF16), ((16 * COARSE_DEV, d), BF16)], limit=1,
        )
        pieces = (picks,)
    else:
        y_rows = lax.ppermute(
            pay, "wide", [(i, (i - 1 if i % 2 == 0 else i + 1) % n_patches) for i in around]
        )
        (far,) = call(
            functools.partial(wrap_kernel, halo), (x_rows, y_rows), [((4 * block, d), BF16)], limit=1
        )
        have = 2
        while True:
            pieces = [known]
            for k in range(1, min(4, n_patches // have)):
                pieces.append(shift(known, k * have))
            have *= len(pieces)
            if have == n_patches:
                break
            (known,) = call(
                join_kernel, pieces, [((len(pieces) * known.shape[0], d), BF16)], limit=2
            )
    coarse_rows = sum(p.shape[0] for p in pieces)

    (base_f,) = call(
        base_kernel, (oh1, table, edge_weight_in, e_bias, fine_edges), [((edges, d), F32)], limit=16
    )
    (out,) = call(
        main_kernel,
        (partner, far, nl, base_f, base_c, oh2, sel, inc, shifts, nu,
         edge_weight_in, edge_weight_out, node_weight_in, node_weight_out,
         e_gain, n_gain, n_shift, *pieces),
        [((nodes, d), BF16)],
        scratch=[
            pltpu.VMEM((table_b, d), BF16),
            pltpu.VMEM((coarse_rows, d), BF16),
            pltpu.VMEM((padded, d), BF16),
            pltpu.VMEM((padded, d), BF16),
        ],
        limit=16,
        far_out=True,
    )
    return out


def solution(mesh):
    axes = ("grp", "wide", "narrow")
    matrix, vector, whole = P(axes, None), P(axes), P()
    return jax.shard_map(
        shards,
        mesh=mesh,
        in_specs=(matrix, matrix, vector, vector, matrix, vector, vector) + (whole,) * 10,
        out_specs=matrix,
        check_vma=False,
    )
```

```python
import functools

import jax
import jax.numpy as jnp
from jax import lax
from jax.experimental import pallas as pl
from jax.experimental.pallas import tpu as pltpu
from jax.sharding import PartitionSpec as P


COARSE_DEV = 4
LANES = 128
CHUNKS = 3
RING = 8
BF16 = jnp.bfloat16
F32 = jnp.float32
MIB = 1 << 20


def silu_of_half(u):
    return u + u * jnp.tanh(u)


def normalized(values):
    center = values - jnp.mean(values, axis=-1, keepdims=True)
    spread = jnp.mean(center * center, axis=-1, keepdims=True)
    return center * lax.rsqrt(spread + 1e-05)


def dot(a, b):
    return jnp.dot(a, b, preferred_element_type=F32)


def columns(row):
    return jnp.broadcast_to(row, (LANES, row.shape[1])).T


def one_hot(cols, width, value=1.0):
    lane = lax.broadcasted_iota(jnp.int32, cols[0].shape, 1)
    blocks = []
    for b in range(width // LANES):
        hit = cols[0] == lane + b * LANES
        for c in cols[1:]:
            hit = hit | (c == lane + b * LANES)
        blocks.append(jnp.where(hit, value, 0.0).astype(BF16))
    return jnp.concatenate(blocks, axis=1)


def stage_kernel(n, *refs):
    sems = refs[-1]
    copies = [pltpu.make_async_copy(refs[k], refs[k - n - 1], sems.at[k]) for k in range(n)]
    for c in copies:
        c.start()
    for c in copies:
        c.wait()


def pay_kernel(halo, nl, partner, pay):
    nodes = nl.shape[0]
    pick = lambda r: jnp.concatenate([r[nodes - halo :, :], r[:COARSE_DEV, :]], axis=0)
    own, other = pick(nl), pick(partner)
    low = lax.axis_index("narrow") == 0
    pay[...] = jnp.concatenate([jnp.where(low, own, other), jnp.where(low, other, own)], axis=0)


def coarse_of(rows, halo):
    block = halo + COARSE_DEV
    return [rows[halo:block, :], rows[block + halo : 2 * block, :]]


def pair_kernel(halo, pay, x_rows, _, known, rich):
    known[...] = jnp.concatenate(coarse_of(pay, halo) + coarse_of(x_rows, halo), axis=0)
    rich[...] = jnp.concatenate([known[...]] + halos_of(x_rows, halo), axis=0)


def both_kernel(first, second, _, __, both):
    n = first.shape[0]
    both[:n, :] = first[...]
    both[n:, :] = second[...]


def halos_of(rows, halo):
    block = halo + COARSE_DEV
    return [rows[:halo, :], rows[block : block + halo, :]]


def collect_kernel(halo, known, both, other, far, picks):
    n, m = 2 * halo, known.shape[0]
    low = lax.axis_index("narrow") == 0
    even = lax.axis_index("wide") % 2 == 0
    zero, one = jnp.where(low, both[...], other[...]), jnp.where(low, other[...], both[...])
    picks[...] = jnp.concatenate([known[...], one[:m], one[m + n :], zero[:m]], axis=0)
    source = jnp.where(even, zero[m : m + n], one[m : m + n])
    far[...] = jnp.concatenate([source, known[: 2 * COARSE_DEV]], axis=0)


def wrap_kernel(halo, y_rows, far):
    far[...] = jnp.concatenate(
        halos_of(y_rows[...], halo) + [y_rows[: 2 * COARSE_DEV, :]], axis=0
    )


def join_kernel(*refs):
    at = 0
    for r in refs[:-1]:
        refs[-1][at : at + r.shape[0], :] = r[...]
        at += r.shape[0]


def places(n_patches):
    wide = lax.axis_index("wide")
    half = lax.axis_index("narrow")
    y_patch = jnp.where(wide % 2 == 0, wide + n_patches - 1, wide + 1) % n_patches
    return wide, half, wide * 2 + half, y_patch


def local_kernel(
    nodes, halo, n_patches,
    nl, fs, fr, cs, cr, e_bias, n_bias, e_shift, ce, w_in, u_in,
    base_c, oh1, oh2, sel, inc, shifts, nu, table,
):
    d = nl.shape[1]
    wide, half, device, y_patch = places(n_patches)
    patch = 2 * nodes
    first = nodes - halo
    block = halo + COARSE_DEV

    recv = fr[...] - device * nodes
    send = fs[...]

    def offset(p):
        off = send - p * patch
        inside = (off >= 0) & (off < patch)
        upper = (off >= nodes).astype(jnp.int32)
        return inside, upper, off - upper * nodes

    inside, upper, loc = offset(wide)
    own = jnp.where(inside & (upper == half), loc + nodes, -1)
    pos = jnp.where(inside & (upper != half), loc, -1)
    for k, p in enumerate((wide ^ 1, y_patch)):
        inside, upper, loc = offset(p)
        at = nodes + k * 2 * block + upper * (block, halo)[k] + loc - first
        pos = jnp.where(inside, at, pos)

    recv_c = cr[...] - device * nodes
    chip_rows = cs[...].astype(F32)
    owner = jnp.floor((chip_rows + 0.5) * (1.0 / nodes)).astype(jnp.int32)
    slot_c = cs[...] - owner * nodes
    patch_c = owner // 2
    if n_patches == RING:
        pairs = n_patches // 2
        place_c = (patch_c // 2 - wide // 2 + pairs) % pairs * 2 + (patch_c ^ wide) % 2
    else:
        place_c = patch_c ^ wide
    pos_c = place_c * (2 * COARSE_DEV) + (owner % 2) * COARSE_DEV + slot_c
    total = fr.shape[1] + cr.shape[1]
    spare = jnp.full((1, inc.shape[1] - total), -1, jnp.int32)
    recv_all = jnp.concatenate([recv, recv_c, spare], axis=1)
    node_at = lax.broadcasted_iota(jnp.int32, inc.shape, 0)
    marks = jnp.where(node_at == recv_all, 1.0, 0.0)
    inc[...] = marks.astype(BF16)
    shifts[...] = jnp.sum(marks, axis=1, keepdims=True) * e_shift[...]
    wide_c = -(-sel.shape[1] // LANES) * LANES
    sel[...] = one_hot((columns(pos_c),), wide_c)[:, : sel.shape[1]]
    oh_c = one_hot((columns(recv_c),), table.shape[0])
    oh1[...] = one_hot((columns(recv), columns(own)), oh1.shape[1], 0.5)
    oh2[...] = one_hot((columns(pos),), oh2.shape[1], 0.5)
    table[2 * nodes :, :] = jnp.zeros_like(table[2 * nodes :, :])

    node_rows = nl[...]
    table[0:nodes, :] = dot(node_rows, w_in[2 * d :, :]).astype(BF16)
    table[nodes : 2 * nodes, :] = dot(node_rows, w_in[d : 2 * d, :]).astype(BF16)
    nu[...] = 0.5 * (dot(node_rows, u_in[:d, :]) + n_bias[...])
    base_c[...] = 0.5 * (dot(ce[...], w_in[:d, :]) + dot(oh_c, table[...]) + e_bias[...])


def base_kernel(oh1, table, w_in, e_bias, fe, base_f):
    d = fe.shape[1]
    own = 0.5 * (dot(fe[...], w_in[:d, :]) + e_bias[...])
    base_f[...] = own + dot(oh1[...], table[...])


def w_send(w_in):
    d = w_in.shape[1]
    return w_in[d : 2 * d, :]


def prep_kernel(partner, x_rows, w_in, ready):
    n = partner.shape[0]
    ready[:n, :] = dot(partner[...], w_send(w_in)).astype(BF16)
    ready[n:, :] = dot(x_rows[...], w_send(w_in)).astype(BF16)


def main_kernel(
    ready, far, nl, base_f, base_c, oh2, sel, inc, shifts, nu, w_in, w_out, u_in, u_out,
    e_gain, n_gain, n_shift, *refs,
):
    pieces, (out, table, picks, hidden, mess) = refs[:-5], refs[-5:]
    picks[...] = jnp.concatenate([r[...] for r in pieces], axis=0)
    a = ready.shape[0]
    w_s = w_send(w_in)
    table[:a, :] = ready[...]
    table[a:, :] = dot(far[...], w_s).astype(BF16)

    rows, coarse = base_f.shape[0], base_c.shape[0]
    step = rows // CHUNKS
    parts = [slice(k * step, (k + 1) * step) for k in range(CHUNKS)] + [slice(rows, rows + coarse)]

    def first(k):
        s = parts[k]
        if k < CHUNKS:
            half = base_f[s, :] + dot(oh2[s, :], table[...])
        else:
            picked = dot(sel[...], picks[...]).astype(BF16)
            half = base_c[...] + 0.5 * dot(picked, w_s)
        hidden[s, :] = silu_of_half(half).astype(BF16)

    def second(k):
        s = parts[k]
        mess[s, :] = normalized(dot(hidden[s, :], w_out[...])).astype(BF16)

    mess[rows + coarse :, :] = jnp.zeros_like(mess[rows + coarse :, :])
    first(CHUNKS)
    first(0)
    for k in range(1, CHUNKS):
        first(k)
        second(k - 1)
    parts[CHUNKS - 1] = slice(parts[CHUNKS - 1].start, rows + coarse)
    second(CHUNKS - 1)
    summed = dot(inc[...], mess[...]) * e_gain[...] + shifts[...]
    d = nl.shape[1]
    half = nu[...] + 0.5 * dot(summed.astype(BF16), u_in[d:, :])
    update = normalized(dot(silu_of_half(half).astype(BF16), u_out[...]))
    out[...] = (nl[...].astype(F32) + (update * n_gain[...] + n_shift[...])).astype(BF16)


NEAR = pl.BlockSpec(memory_space=pltpu.VMEM)
FAR = pl.BlockSpec(memory_space=pltpu.HBM)


def near(*arrays):
    return [pltpu.with_memory_space_constraint(a, pltpu.VMEM) for a in arrays]


def call(kernel, near_in, outs, far_in=(), scratch=(), limit=8, far_out=False, cost=None):
    outs = [(o.shape, o.dtype) if hasattr(o, "shape") else o for o in outs]
    kind = (lambda s, t: jax.ShapeDtypeStruct(s, t)) if far_out else (lambda s, t: pltpu.VMEM(s, t))
    return pl.pallas_call(
        kernel,
        out_shape=tuple(kind(*o) for o in outs),
        in_specs=[NEAR] * len(near_in) + [FAR] * len(far_in),
        out_specs=tuple([NEAR] * len(outs)),
        scratch_shapes=list(scratch),
        compiler_params=pltpu.CompilerParams(vmem_limit_bytes=limit * MIB),
        cost_estimate=pl.CostEstimate(flops=cost or 0, bytes_accessed=cost or 0, transcendentals=0),
    )(*near(*near_in), *[pltpu.with_memory_space_constraint(a, pltpu.HBM) for a in far_in])


def shards(
    node_latent, fine_edges, fine_senders, fine_receivers, coarse_edges, coarse_senders,
    coarse_receivers, edge_weight_in, edge_bias, edge_weight_out, edge_gain, edge_shift,
    node_weight_in, node_bias, node_weight_out, node_gain, node_shift,
):
    nodes, d = node_latent.shape
    halo = nodes // 8
    block = halo + COARSE_DEV
    n_patches = lax.axis_size("wide")
    edges, coarse_count = fine_edges.shape[0], coarse_edges.shape[0]
    small = [node_latent] + [
        v.reshape(1, -1)
        for v in (
            fine_senders, fine_receivers, coarse_senders, coarse_receivers, edge_bias, node_bias,
            edge_gain, edge_shift, node_gain, node_shift,
        )
    ]
    dma = pltpu.SemaphoreType.DMA

    partner = lax.ppermute(node_latent, "narrow", [(0, 1), (1, 0)])
    nl, fs, fr, cs, cr, e_bias, n_bias, e_gain, e_shift, n_gain, n_shift = call(
        functools.partial(stage_kernel, len(small)), (), small,
        far_in=small + [fine_edges, edge_weight_in, node_weight_in], scratch=[dma((len(small),))], limit=1
    )
    (pay,) = call(functools.partial(pay_kernel, halo), (nl, partner), [((2 * block, d), BF16)], limit=1)
    around = range(n_patches)
    table_a = -(-2 * nodes // LANES) * LANES
    table_b = nodes + 4 * block
    padded = -(-(edges + coarse_count) // LANES) * LANES
    base_c, oh1, oh2, sel, inc, shifts, nu, table = call(
        functools.partial(local_kernel, nodes, halo, n_patches),
        (nl, fs, fr, cs, cr, e_bias, n_bias, e_shift, coarse_edges, edge_weight_in, node_weight_in),
        [
            ((coarse_count, d), F32),
            ((edges, table_a), BF16),
            ((edges, table_b), BF16),
            ((coarse_count, 2 * n_patches * COARSE_DEV), BF16),
            ((nodes, padded), BF16),
            ((nodes, d), F32),
            ((nodes, d), F32),
            ((table_a, d), BF16),
        ],
        limit=16,
    )
    shift = lambda v, k: lax.ppermute(v, "wide", [(i, i ^ k) for i in around])
    x_rows = shift(pay, 1)
    known, rich = call(
        functools.partial(pair_kernel, halo), (pay, x_rows, base_c),
        [((4 * COARSE_DEV, d), BF16), ((4 * COARSE_DEV + 2 * halo, d), BF16)], limit=1,
    )
    (base_f,) = call(
        base_kernel, (oh1, table, edge_weight_in, e_bias, fine_edges), [((edges, d), F32)], limit=16
    )
    (ready,) = call(
        prep_kernel, (partner, x_rows, edge_weight_in), [((nodes + 2 * block, d), BF16)], limit=4
    )
    if n_patches == RING:
        spot = lambda p, c: p % n_patches * 2 + c
        split = lambda v, steps: lax.ppermute(
            v, ("wide", "narrow"),
            [(spot(p, c), spot(steps[c](p), c)) for p in around for c in range(2)],
        )
        first = split(rich, (lambda p: p + 2, lambda p: p - 2))
        second = split(known, (lambda p: p ^ 1, lambda p: p + 4))
        (both,) = call(
            both_kernel, (first, second, base_f, ready), [((8 * COARSE_DEV + 2 * halo, d), BF16)], limit=1
        )
        other = lax.ppermute(both, "narrow", [(0, 1), (1, 0)])
        far, picks = call(
            functools.partial(collect_kernel, halo), (known, both, other),
            [((2 * block, d), BF16), ((16 * COARSE_DEV, d), BF16)], limit=1,
        )
        pieces = (picks,)
    else:
        y_rows = lax.ppermute(
            pay, "wide", [(i, (i - 1 if i % 2 == 0 else i + 1) % n_patches) for i in around]
        )
        (far,) = call(
            functools.partial(wrap_kernel, halo), (y_rows,), [((2 * block, d), BF16)], limit=1
        )
        have = 2
        while True:
            pieces = [known]
            for k in range(1, min(4, n_patches // have)):
                pieces.append(shift(known, k * have))
            have *= len(pieces)
            if have == n_patches:
                break
            (known,) = call(
                join_kernel, pieces, [((len(pieces) * known.shape[0], d), BF16)], limit=2
            )
    coarse_rows = sum(p.shape[0] for p in pieces)

    (out,) = call(
        main_kernel,
        (ready, far, nl, base_f, base_c, oh2, sel, inc, shifts, nu,
         edge_weight_in, edge_weight_out, node_weight_in, node_weight_out,
         e_gain, n_gain, n_shift, *pieces),
        [((nodes, d), BF16)],
        scratch=[
            pltpu.VMEM((table_b, d), BF16),
            pltpu.VMEM((coarse_rows, d), BF16),
            pltpu.VMEM((padded, d), BF16),
            pltpu.VMEM((padded, d), BF16),
        ],
        limit=16,
        far_out=True,
    )
    return out


def solution(mesh):
    axes = ("grp", "wide", "narrow")
    matrix, vector, whole = P(axes, None), P(axes), P()
    return jax.shard_map(
        shards,
        mesh=mesh,
        in_specs=(matrix, matrix, vector, vector, matrix, vector, vector) + (whole,) * 10,
        out_specs=matrix,
        check_vma=False,
    )
```

```python
import functools

import jax
import jax.numpy as jnp
from jax import lax
from jax.experimental import pallas as pl
from jax.experimental.pallas import tpu as pltpu
from jax.sharding import PartitionSpec as P


COARSE_DEV = 4
LANES = 128
CHUNKS = 3
LATE = 128
RING = 8
BF16 = jnp.bfloat16
F32 = jnp.float32
MIB = 1 << 20


def silu_of_half(u):
    return u + u * jnp.tanh(u)


def normalized(values):
    center = values - jnp.mean(values, axis=-1, keepdims=True)
    spread = jnp.mean(center * center, axis=-1, keepdims=True)
    return center * lax.rsqrt(spread + 1e-05)


def dot(a, b):
    return jnp.dot(a, b, preferred_element_type=F32)


def columns(row):
    return jnp.broadcast_to(row, (LANES, row.shape[1])).T


def one_hot(cols, width, value=1.0):
    lane = lax.broadcasted_iota(jnp.int32, cols[0].shape, 1)
    blocks = []
    for b in range(width // LANES):
        hit = cols[0] == lane + b * LANES
        for c in cols[1:]:
            hit = hit | (c == lane + b * LANES)
        blocks.append(jnp.where(hit, value, 0.0).astype(BF16))
    return jnp.concatenate(blocks, axis=1)


def stage_kernel(n, *refs):
    sems = refs[-1]
    copies = [pltpu.make_async_copy(refs[k], refs[k - n - 1], sems.at[k]) for k in range(n)]
    for c in copies:
        c.start()
    for c in copies:
        c.wait()


def pay_kernel(halo, nl, partner, pay):
    nodes = nl.shape[0]
    pick = lambda r: jnp.concatenate([r[nodes - halo :, :], r[:COARSE_DEV, :]], axis=0)
    own, other = pick(nl), pick(partner)
    low = lax.axis_index("narrow") == 0
    pay[...] = jnp.concatenate([jnp.where(low, own, other), jnp.where(low, other, own)], axis=0)


def coarse_of(rows, halo):
    block = halo + COARSE_DEV
    return [rows[halo:block, :], rows[block + halo : 2 * block, :]]


def pair_kernel(halo, pay, x_rows, _, known, rich):
    known[...] = jnp.concatenate(coarse_of(pay, halo) + coarse_of(x_rows, halo), axis=0)
    rich[...] = jnp.concatenate([known[...]] + halos_of(x_rows, halo), axis=0)


def both_kernel(first, second, _, __, both):
    n = first.shape[0]
    both[:n, :] = first[...]
    both[n:, :] = second[...]


def halos_of(rows, halo):
    block = halo + COARSE_DEV
    return [rows[:halo, :], rows[block : block + halo, :]]


def collect_kernel(halo, known, both, other, far, picks):
    n, m = 2 * halo, known.shape[0]
    low = lax.axis_index("narrow") == 0
    even = lax.axis_index("wide") % 2 == 0
    zero, one = jnp.where(low, both[...], other[...]), jnp.where(low, other[...], both[...])
    picks[...] = jnp.concatenate([known[...], one[:m], one[m + n :], zero[:m]], axis=0)
    source = jnp.where(even, zero[m : m + n], one[m : m + n])
    far[...] = jnp.concatenate([source, known[: 2 * COARSE_DEV]], axis=0)


def wrap_kernel(halo, y_rows, far):
    far[...] = jnp.concatenate(
        halos_of(y_rows[...], halo) + [y_rows[: 2 * COARSE_DEV, :]], axis=0
    )


def join_kernel(*refs):
    at = 0
    for r in refs[:-1]:
        refs[-1][at : at + r.shape[0], :] = r[...]
        at += r.shape[0]


def places(n_patches):
    wide = lax.axis_index("wide")
    half = lax.axis_index("narrow")
    y_patch = jnp.where(wide % 2 == 0, wide + n_patches - 1, wide + 1) % n_patches
    return wide, half, wide * 2 + half, y_patch


def local_kernel(
    nodes, halo, n_patches,
    nl, fs, fr, cs, cr, e_bias, n_bias, e_shift, ce, w_in, u_in,
    base_c, oh1, oh2, sel, inc_f, inc_e, inc_l, inc_c, pack, late, shifts, nu, table,
):
    d = nl.shape[1]
    wide, half, device, y_patch = places(n_patches)
    patch = 2 * nodes
    first = nodes - halo
    block = halo + COARSE_DEV

    recv = fr[...] - device * nodes
    send = fs[...]

    def offset(p):
        off = send - p * patch
        inside = (off >= 0) & (off < patch)
        upper = (off >= nodes).astype(jnp.int32)
        return inside, upper, off - upper * nodes

    inside, upper, loc = offset(wide)
    own = jnp.where(inside & (upper == half), loc + nodes, -1)
    pos = jnp.where(inside & (upper != half), loc, -1)
    for k, p in enumerate((wide ^ 1, y_patch)):
        inside, upper, loc = offset(p)
        at = nodes + k * 2 * block + upper * (block, halo)[k] + loc - first
        pos = jnp.where(inside, at, pos)

    recv_c = cr[...] - device * nodes
    chip_rows = cs[...].astype(F32)
    owner = jnp.floor((chip_rows + 0.5) * (1.0 / nodes)).astype(jnp.int32)
    slot_c = cs[...] - owner * nodes
    patch_c = owner // 2
    if n_patches == RING:
        pairs = n_patches // 2
        place_c = (patch_c // 2 - wide // 2 + pairs) % pairs * 2 + (patch_c ^ wide) % 2
    else:
        place_c = patch_c ^ wide
    pos_c = place_c * (2 * COARSE_DEV) + (owner % 2) * COARSE_DEV + slot_c

    def incidence(ids):
        at = lax.broadcasted_iota(jnp.int32, (nodes, ids.shape[1]), 0)
        return jnp.where(at == ids, 1.0, 0.0)

    edges = fr.shape[1]
    last_block = pos >= nodes + 2 * block
    late_row = jnp.where(last_block, 1.0, 0.0)
    before = lax.broadcasted_iota(jnp.int32, (edges, edges), 0)
    before = before < lax.broadcasted_iota(jnp.int32, (edges, edges), 1)
    flags = jnp.broadcast_to(late_row, (8, edges)).astype(BF16)
    rank = dot(flags, jnp.where(before, 1.0, 0.0).astype(BF16))[0:1, :].astype(jnp.int32)
    rank = jnp.where(last_block, rank, -1)
    chosen = lax.broadcasted_iota(jnp.int32, pack.shape, 0) == rank
    chosen = jnp.where(chosen, 1.0, 0.0).astype(BF16)
    pack[...] = chosen
    late[...] = late_row
    marks, marks_c = incidence(recv), incidence(recv_c)
    inc_f[...] = marks.astype(BF16)
    inc_e[...] = (marks * (1.0 - late_row)).astype(BF16)
    inc_l[...] = lax.dot_general(
        marks.astype(BF16), chosen, (((1,), (1,)), ((), ())), preferred_element_type=F32
    ).astype(BF16)
    inc_c[...] = marks_c.astype(BF16)
    count = jnp.sum(marks, axis=1, keepdims=True) + jnp.sum(marks_c, axis=1, keepdims=True)
    shifts[...] = count * e_shift[...]
    wide_c = -(-sel.shape[1] // LANES) * LANES
    sel[...] = one_hot((columns(pos_c),), wide_c)[:, : sel.shape[1]]
    oh_c = one_hot((columns(recv_c),), table.shape[0])
    oh1[...] = one_hot((columns(recv), columns(own)), oh1.shape[1], 0.5)
    oh2[...] = one_hot((columns(pos),), oh2.shape[1], 0.5)
    table[2 * nodes :, :] = jnp.zeros_like(table[2 * nodes :, :])

    node_rows = nl[...]
    table[0:nodes, :] = dot(node_rows, w_in[2 * d :, :]).astype(BF16)
    table[nodes : 2 * nodes, :] = dot(node_rows, w_in[d : 2 * d, :]).astype(BF16)
    nu[...] = 0.5 * (dot(node_rows, u_in[:d, :]) + n_bias[...])
    base_c[...] = 0.5 * (dot(ce[...], w_in[:d, :]) + dot(oh_c, table[...]) + e_bias[...])


def base_kernel(oh1, table, w_in, e_bias, fe, _, __, base_f):
    d = fe.shape[1]
    own = 0.5 * (dot(fe[...], w_in[:d, :]) + e_bias[...])
    base_f[...] = own + dot(oh1[...], table[...])


def w_send(w_in):
    d = w_in.shape[1]
    return w_in[d : 2 * d, :]


def prep_kernel(partner, x_rows, base_f, oh2, pack, w_in, ready, hidden, late_half, late_oh):
    n = partner.shape[0]
    m = n + x_rows.shape[0]
    ready[:n, :] = dot(partner[...], w_send(w_in)).astype(BF16)
    ready[n:m, :] = dot(x_rows[...], w_send(w_in)).astype(BF16)
    ready[m:, :] = jnp.zeros_like(ready[m:, :])
    half = base_f[...]
    hidden[...] = silu_of_half(half + dot(oh2[...], ready[...])).astype(BF16)
    coarse_bits = half.astype(BF16)
    fine_bits = (half - coarse_bits.astype(F32)).astype(BF16)
    late_half[...] = dot(pack[...], coarse_bits) + dot(pack[...], fine_bits)
    late_oh[...] = dot(pack[...], oh2[:, oh2.shape[1] - LANES :]).astype(BF16)


def early_kernel(hidden, inc_e, w_out, total, mess):
    rows = hidden.shape[0]
    step = rows // CHUNKS
    for k in range(CHUNKS):
        s = slice(k * step, (k + 1) * step)
        mess[s, :] = normalized(dot(hidden[s, :], w_out[...])).astype(BF16)
    total[...] = dot(inc_e[...], mess[...])


def last_kernel(
    n_pieces, ready, far, nl, base_f, base_c, oh2, sel, inc_f, inc_l, inc_c, late, late_half, late_oh,
    total, shifts, nu, w_in, w_out, u_in, u_out, e_gain, n_gain, n_shift, *refs,
):
    pieces, (out, picks, table, hidden, mess, acc) = refs[:n_pieces], refs[n_pieces:]
    w_s = w_send(w_in)
    a = ready.shape[0] - far.shape[0]
    table[:a, :] = ready[:a, :]
    table[a:, :] = dot(far[...], w_s).astype(BF16)
    picks[...] = jnp.concatenate([r[...] for r in pieces], axis=0)
    picked = dot(sel[...], picks[...]).astype(BF16)
    n = late_half.shape[0]
    tail = table[table.shape[0] - LANES :, :]
    half = jnp.concatenate(
        [late_half[...] + dot(late_oh[...], tail), base_c[...] + 0.5 * dot(picked, w_s)], axis=0
    )
    some = normalized(dot(silu_of_half(half).astype(BF16), w_out[...])).astype(BF16)
    coarse_sum = dot(inc_c[...], some[n:])
    acc[...] = total[...] + dot(inc_l[...], some[:n]) + coarse_sum

    @pl.when(jnp.sum(late[...]) > n)
    def _():
        rows = base_f.shape[0]
        step = rows // CHUNKS
        for k in range(CHUNKS):
            s = slice(k * step, (k + 1) * step)
            hidden[s, :] = silu_of_half(base_f[s, :] + dot(oh2[s, :], table[...])).astype(BF16)
            mess[s, :] = normalized(dot(hidden[s, :], w_out[...])).astype(BF16)
        acc[...] = dot(inc_f[...], mess[...]) + coarse_sum

    summed = acc[...] * e_gain[...] + shifts[...]
    d = nl.shape[1]
    half = nu[...] + 0.5 * dot(summed.astype(BF16), u_in[d:, :])
    update = normalized(dot(silu_of_half(half).astype(BF16), u_out[...]))
    out[...] = (nl[...].astype(F32) + (update * n_gain[...] + n_shift[...])).astype(BF16)


NEAR = pl.BlockSpec(memory_space=pltpu.VMEM)
FAR = pl.BlockSpec(memory_space=pltpu.HBM)


def near(*arrays):
    return [pltpu.with_memory_space_constraint(a, pltpu.VMEM) for a in arrays]


def call(kernel, near_in, outs, far_in=(), scratch=(), limit=8, far_out=False, cost=None):
    outs = [(o.shape, o.dtype) if hasattr(o, "shape") else o for o in outs]
    kind = (lambda s, t: jax.ShapeDtypeStruct(s, t)) if far_out else (lambda s, t: pltpu.VMEM(s, t))
    return pl.pallas_call(
        kernel,
        out_shape=tuple(kind(*o) for o in outs),
        in_specs=[NEAR] * len(near_in) + [FAR] * len(far_in),
        out_specs=tuple([NEAR] * len(outs)),
        scratch_shapes=list(scratch),
        compiler_params=pltpu.CompilerParams(vmem_limit_bytes=limit * MIB),
        cost_estimate=pl.CostEstimate(flops=cost or 0, bytes_accessed=cost or 0, transcendentals=0),
    )(*near(*near_in), *[pltpu.with_memory_space_constraint(a, pltpu.HBM) for a in far_in])


def shards(
    node_latent, fine_edges, fine_senders, fine_receivers, coarse_edges, coarse_senders,
    coarse_receivers, edge_weight_in, edge_bias, edge_weight_out, edge_gain, edge_shift,
    node_weight_in, node_bias, node_weight_out, node_gain, node_shift,
):
    nodes, d = node_latent.shape
    halo = nodes // 8
    block = halo + COARSE_DEV
    n_patches = lax.axis_size("wide")
    edges, coarse_count = fine_edges.shape[0], coarse_edges.shape[0]
    small = [node_latent] + [
        v.reshape(1, -1)
        for v in (
            fine_senders, fine_receivers, coarse_senders, coarse_receivers, edge_bias, node_bias,
            edge_gain, edge_shift, node_gain, node_shift,
        )
    ]
    dma = pltpu.SemaphoreType.DMA

    partner = lax.ppermute(node_latent, "narrow", [(0, 1), (1, 0)])
    nl, fs, fr, cs, cr, e_bias, n_bias, e_gain, e_shift, n_gain, n_shift = call(
        functools.partial(stage_kernel, len(small)), (), small,
        far_in=small + [fine_edges, edge_weight_in, node_weight_in], scratch=[dma((len(small),))], limit=1
    )
    (pay,) = call(functools.partial(pay_kernel, halo), (nl, partner), [((2 * block, d), BF16)], limit=1)
    around = range(n_patches)
    table_a = -(-2 * nodes // LANES) * LANES
    table_b = nodes + 4 * block
    base_c, oh1, oh2, sel, inc_f, inc_e, inc_l, inc_c, pack, late, shifts, nu, table = call(
        functools.partial(local_kernel, nodes, halo, n_patches),
        (nl, fs, fr, cs, cr, e_bias, n_bias, e_shift, coarse_edges, edge_weight_in, node_weight_in),
        [
            ((coarse_count, d), F32),
            ((edges, table_a), BF16),
            ((edges, table_b), BF16),
            ((coarse_count, 2 * n_patches * COARSE_DEV), BF16),
            ((nodes, edges), BF16),
            ((nodes, edges), BF16),
            ((nodes, LATE), BF16),
            ((nodes, coarse_count), BF16),
            ((LATE, edges), BF16),
            ((1, edges), F32),
            ((nodes, d), F32),
            ((nodes, d), F32),
            ((table_a, d), BF16),
        ],
        limit=16,
    )
    shift = lambda v, k: lax.ppermute(v, "wide", [(i, i ^ k) for i in around])
    x_rows = shift(pay, 1)
    known, rich = call(
        functools.partial(pair_kernel, halo), (pay, x_rows, base_c),
        [((4 * COARSE_DEV, d), BF16), ((4 * COARSE_DEV + 2 * halo, d), BF16)], limit=1,
    )
    (base_f,) = call(
        base_kernel,
        (oh1, table, edge_weight_in, e_bias, fine_edges, edge_weight_out, node_weight_out),
        [((edges, d), F32)],
        limit=16,
    )
    ready, hidden, late_half, late_oh = call(
        prep_kernel, (partner, x_rows, base_f, oh2, pack, edge_weight_in),
        [((table_b, d), BF16), ((edges, d), BF16), ((LATE, d), F32), ((LATE, LANES), BF16)],
        limit=12,
    )
    if n_patches == RING:
        spot = lambda p, c: p % n_patches * 2 + c
        split = lambda v, steps: lax.ppermute(
            v, ("wide", "narrow"),
            [(spot(p, c), spot(steps[c](p), c)) for p in around for c in range(2)],
        )
        first = split(rich, (lambda p: p + 2, lambda p: p - 2))
        second = split(known, (lambda p: p ^ 1, lambda p: p + 4))
        (both,) = call(
            both_kernel, (first, second, base_f, ready), [((8 * COARSE_DEV + 2 * halo, d), BF16)], limit=1
        )
        other = lax.ppermute(both, "narrow", [(0, 1), (1, 0)])
        far, picks = call(
            functools.partial(collect_kernel, halo), (known, both, other),
            [((2 * block, d), BF16), ((16 * COARSE_DEV, d), BF16)], limit=1,
        )
        pieces = (picks,)
    else:
        y_rows = lax.ppermute(
            pay, "wide", [(i, (i - 1 if i % 2 == 0 else i + 1) % n_patches) for i in around]
        )
        (far,) = call(
            functools.partial(wrap_kernel, halo), (y_rows,), [((2 * block, d), BF16)], limit=1
        )
        have = 2
        while True:
            pieces = [known]
            for k in range(1, min(4, n_patches // have)):
                pieces.append(shift(known, k * have))
            have *= len(pieces)
            if have == n_patches:
                break
            (known,) = call(
                join_kernel, pieces, [((len(pieces) * known.shape[0], d), BF16)], limit=2
            )
    coarse_rows = sum(p.shape[0] for p in pieces)

    (total,) = call(
        early_kernel, (hidden, inc_e, edge_weight_out), [((nodes, d), F32)],
        scratch=[pltpu.VMEM((edges, d), BF16)], limit=12,
    )
    (out,) = call(
        functools.partial(last_kernel, len(pieces)),
        (ready, far, nl, base_f, base_c, oh2, sel, inc_f, inc_l, inc_c, late, late_half, late_oh, total,
         shifts, nu, edge_weight_in, edge_weight_out, node_weight_in, node_weight_out,
         e_gain, n_gain, n_shift, *pieces),
        [((nodes, d), BF16)],
        scratch=[
            pltpu.VMEM((coarse_rows, d), BF16),
            pltpu.VMEM((table_b, d), BF16),
            pltpu.VMEM((edges, d), BF16),
            pltpu.VMEM((edges, d), BF16),
            pltpu.VMEM((nodes, d), F32),
        ],
        limit=16,
        far_out=True,
    )
    return out


def solution(mesh):
    axes = ("grp", "wide", "narrow")
    matrix, vector, whole = P(axes, None), P(axes), P()
    return jax.shard_map(
        shards,
        mesh=mesh,
        in_specs=(matrix, matrix, vector, vector, matrix, vector, vector) + (whole,) * 10,
        out_specs=matrix,
        check_vma=False,
    )
```

```python
import functools

import jax
import jax.numpy as jnp
from jax import lax
from jax.experimental import pallas as pl
from jax.experimental.pallas import tpu as pltpu
from jax.sharding import PartitionSpec as P


COARSE_DEV = 4
LANES = 128
CHUNKS = 3
LATE = 128
RING = 8
BF16 = jnp.bfloat16
F32 = jnp.float32
MIB = 1 << 20


def silu_of_half(u):
    return u + u * jnp.tanh(u)


def normalized(values):
    center = values - jnp.mean(values, axis=-1, keepdims=True)
    spread = jnp.mean(center * center, axis=-1, keepdims=True)
    return center * lax.rsqrt(spread + 1e-05)


def dot(a, b):
    return jnp.dot(a, b, preferred_element_type=F32)


def columns(row):
    return jnp.broadcast_to(row, (LANES, row.shape[1])).T


def one_hot(cols, width, value=1.0):
    lane = lax.broadcasted_iota(jnp.int32, cols[0].shape, 1)
    blocks = []
    for b in range(width // LANES):
        hit = cols[0] == lane + b * LANES
        for c in cols[1:]:
            hit = hit | (c == lane + b * LANES)
        blocks.append(jnp.where(hit, value, 0.0).astype(BF16))
    return jnp.concatenate(blocks, axis=1)


def stage_kernel(n, *refs):
    sems = refs[-1]
    copies = [pltpu.make_async_copy(refs[k], refs[k - n - 1], sems.at[k]) for k in range(n)]
    for c in copies:
        c.start()
    for c in copies:
        c.wait()


def pay_kernel(halo, nl, partner, pay):
    nodes = nl.shape[0]
    pick = lambda r: jnp.concatenate([r[nodes - halo :, :], r[:COARSE_DEV, :]], axis=0)
    own, other = pick(nl), pick(partner)
    low = lax.axis_index("narrow") == 0
    pay[...] = jnp.concatenate([jnp.where(low, own, other), jnp.where(low, other, own)], axis=0)


def coarse_of(rows, halo):
    block = halo + COARSE_DEV
    return [rows[halo:block, :], rows[block + halo : 2 * block, :]]


def pair_kernel(halo, pay, x_rows, _, known, rich):
    known[...] = jnp.concatenate(coarse_of(pay, halo) + coarse_of(x_rows, halo), axis=0)
    rich[...] = jnp.concatenate([known[...]] + halos_of(x_rows, halo), axis=0)


def both_kernel(first, second, _, __, both):
    n = first.shape[0]
    both[:n, :] = first[...]
    both[n:, :] = second[...]


def halos_of(rows, halo):
    block = halo + COARSE_DEV
    return [rows[:halo, :], rows[block : block + halo, :]]


def collect_kernel(halo, known, both, other, far, picks):
    n, m = 2 * halo, known.shape[0]
    low = lax.axis_index("narrow") == 0
    even = lax.axis_index("wide") % 2 == 0
    zero, one = jnp.where(low, both[...], other[...]), jnp.where(low, other[...], both[...])
    picks[...] = jnp.concatenate([known[...], one[:m], one[m + n :], zero[:m]], axis=0)
    source = jnp.where(even, zero[m : m + n], one[m : m + n])
    far[...] = jnp.concatenate([source, known[: 2 * COARSE_DEV]], axis=0)


def wrap_kernel(halo, y_rows, far):
    far[...] = jnp.concatenate(
        halos_of(y_rows[...], halo) + [y_rows[: 2 * COARSE_DEV, :]], axis=0
    )


def join_kernel(*refs):
    at = 0
    for r in refs[:-1]:
        refs[-1][at : at + r.shape[0], :] = r[...]
        at += r.shape[0]


def places(n_patches):
    wide = lax.axis_index("wide")
    half = lax.axis_index("narrow")
    y_patch = jnp.where(wide % 2 == 0, wide + n_patches - 1, wide + 1) % n_patches
    return wide, half, wide * 2 + half, y_patch


def local_kernel(
    nodes, halo, n_patches,
    nl, fs, fr, cs, cr, e_bias, n_bias, e_shift, ce, w_in, u_in,
    base_c, oh1, oh2, sel, inc_f, inc_e, inc_l, pack, late, shifts, nu, table,
):
    d = nl.shape[1]
    wide, half, device, y_patch = places(n_patches)
    patch = 2 * nodes
    first = nodes - halo
    block = halo + COARSE_DEV

    recv = fr[...] - device * nodes
    send = fs[...]

    def offset(p):
        off = send - p * patch
        inside = (off >= 0) & (off < patch)
        upper = (off >= nodes).astype(jnp.int32)
        return inside, upper, off - upper * nodes

    inside, upper, loc = offset(wide)
    own = jnp.where(inside & (upper == half), loc + nodes, -1)
    pos = jnp.where(inside & (upper != half), loc, -1)
    for k, p in enumerate((wide ^ 1, y_patch)):
        inside, upper, loc = offset(p)
        at = nodes + k * 2 * block + upper * (block, halo)[k] + loc - first
        pos = jnp.where(inside, at, pos)

    recv_c = cr[...] - device * nodes
    chip_rows = cs[...].astype(F32)
    owner = jnp.floor((chip_rows + 0.5) * (1.0 / nodes)).astype(jnp.int32)
    slot_c = cs[...] - owner * nodes
    patch_c = owner // 2
    if n_patches == RING:
        pairs = n_patches // 2
        place_c = (patch_c // 2 - wide // 2 + pairs) % pairs * 2 + (patch_c ^ wide) % 2
    else:
        place_c = patch_c ^ wide
    pos_c = place_c * (2 * COARSE_DEV) + (owner % 2) * COARSE_DEV + slot_c

    def incidence(ids):
        at = lax.broadcasted_iota(jnp.int32, (nodes, ids.shape[1]), 0)
        return jnp.where(at == ids, 1.0, 0.0)

    edges = fr.shape[1]
    last_block = pos >= nodes + 2 * block
    late_row = jnp.where(last_block, 1.0, 0.0)
    before = lax.broadcasted_iota(jnp.int32, (edges, edges), 0)
    before = before < lax.broadcasted_iota(jnp.int32, (edges, edges), 1)
    flags = jnp.broadcast_to(late_row, (8, edges)).astype(BF16)
    rank = dot(flags, jnp.where(before, 1.0, 0.0).astype(BF16))[0:1, :].astype(jnp.int32)
    rank = jnp.where(last_block, rank, -1)
    chosen = lax.broadcasted_iota(jnp.int32, pack.shape, 0) == rank
    chosen = jnp.where(chosen, 1.0, 0.0).astype(BF16)
    pack[...] = chosen
    over = jnp.sum(late_row, axis=1, keepdims=True) > LATE
    late[...] = jnp.broadcast_to(jnp.where(over, 1.0, 0.0), late.shape)
    marks, marks_c = incidence(recv), incidence(recv_c)
    inc_f[...] = marks.astype(BF16)
    inc_e[...] = (marks * (1.0 - late_row)).astype(BF16)
    inc_l[:, :LATE] = lax.dot_general(
        marks.astype(BF16), chosen, (((1,), (1,)), ((), ())), preferred_element_type=F32
    ).astype(BF16)
    inc_l[:, LATE:] = marks_c.astype(BF16)
    count = jnp.sum(marks, axis=1, keepdims=True) + jnp.sum(marks_c, axis=1, keepdims=True)
    shifts[...] = count * e_shift[...]
    wide_c = -(-sel.shape[1] // LANES) * LANES
    sel[...] = one_hot((columns(pos_c),), wide_c, 0.5)[:, : sel.shape[1]]
    oh_c = one_hot((columns(recv_c),), table.shape[0])
    oh1[...] = one_hot((columns(recv), columns(own)), oh1.shape[1], 0.5)
    oh2[...] = one_hot((columns(pos),), oh2.shape[1], 0.5)
    table[2 * nodes :, :] = jnp.zeros_like(table[2 * nodes :, :])

    node_rows = nl[...]
    table[0:nodes, :] = dot(node_rows, w_in[2 * d :, :]).astype(BF16)
    table[nodes : 2 * nodes, :] = dot(node_rows, w_in[d : 2 * d, :]).astype(BF16)
    nu[...] = 0.5 * (dot(node_rows, u_in[:d, :]) + n_bias[...])
    base_c[...] = 0.5 * (dot(ce[...], w_in[:d, :]) + dot(oh_c, table[...]) + e_bias[...])


def base_kernel(oh1, table, w_in, e_bias, fe, _, __, base_f):
    d = fe.shape[1]
    own = 0.5 * (dot(fe[...], w_in[:d, :]) + e_bias[...])
    base_f[...] = own + dot(oh1[...], table[...])


def w_send(w_in):
    d = w_in.shape[1]
    return w_in[d : 2 * d, :]


def prep_kernel(partner, x_rows, base_f, base_c, oh2, sel, pack, w_in, ready, hidden, part, pick):
    n = partner.shape[0]
    m = n + x_rows.shape[0]
    ready[:n, :] = dot(partner[...], w_send(w_in)).astype(BF16)
    ready[n:m, :] = dot(x_rows[...], w_send(w_in)).astype(BF16)
    ready[m:, :] = jnp.zeros_like(ready[m:, :])
    half = base_f[...]
    hidden[...] = silu_of_half(half + dot(oh2[...], ready[...])).astype(BF16)
    coarse_bits = half.astype(BF16)
    fine_bits = (half - coarse_bits.astype(F32)).astype(BF16)
    late = pack.shape[0]
    part[:late, :] = dot(pack[...], coarse_bits) + dot(pack[...], fine_bits)
    part[late:, :] = base_c[...]
    pick[...] = jnp.zeros_like(pick)
    pick[:late, :LANES] = dot(pack[...], oh2[:, oh2.shape[1] - LANES :]).astype(BF16)
    pick[late:, LANES:] = sel[...]


def early_kernel(hidden, inc_e, w_out, total, mess):
    rows = hidden.shape[0]
    step = rows // CHUNKS
    for k in range(CHUNKS):
        s = slice(k * step, (k + 1) * step)
        mess[s, :] = normalized(dot(hidden[s, :], w_out[...])).astype(BF16)
    total[...] = dot(inc_e[...], mess[...])


def last_kernel(
    n_pieces, ready, far, nl, base_f, part, pick, oh2, inc_f, inc_l, late,
    total, shifts, nu, w_in, w_out, u_in, u_out, e_gain, n_gain, n_shift, *refs,
):
    pieces, (out, rows, table, hidden, mess, acc) = refs[:n_pieces], refs[n_pieces:]
    w_s = w_send(w_in)
    a = LANES - far.shape[0]
    rows[:a, :] = jnp.zeros_like(rows[:a, :])
    rows[a:LANES, :] = far[...]
    rows[LANES:, :] = jnp.concatenate([r[...] for r in pieces], axis=0)
    picked = dot(pick[...], rows[...]).astype(BF16)
    half = part[...] + dot(picked, w_s)
    some = normalized(dot(silu_of_half(half).astype(BF16), w_out[...])).astype(BF16)
    acc[...] = total[...] + dot(inc_l[...], some)

    @pl.when(late[0, 0] > 0)
    def _():
        a = ready.shape[0] - far.shape[0]
        table[:a, :] = ready[:a, :]
        table[a:, :] = dot(far[...], w_s).astype(BF16)
        step = base_f.shape[0] // CHUNKS
        for k in range(CHUNKS):
            s = slice(k * step, (k + 1) * step)
            hidden[s, :] = silu_of_half(base_f[s, :] + dot(oh2[s, :], table[...])).astype(BF16)
            mess[s, :] = normalized(dot(hidden[s, :], w_out[...])).astype(BF16)
        acc[...] = dot(inc_f[...], mess[...]) + dot(inc_l[:, LATE:], some[LATE:])

    summed = acc[...] * e_gain[...] + shifts[...]
    d = nl.shape[1]
    half = nu[...] + 0.5 * dot(summed.astype(BF16), u_in[d:, :])
    update = normalized(dot(silu_of_half(half).astype(BF16), u_out[...]))
    out[...] = (nl[...].astype(F32) + (update * n_gain[...] + n_shift[...])).astype(BF16)


NEAR = pl.BlockSpec(memory_space=pltpu.VMEM)
FAR = pl.BlockSpec(memory_space=pltpu.HBM)


def near(*arrays):
    return [pltpu.with_memory_space_constraint(a, pltpu.VMEM) for a in arrays]


def call(kernel, near_in, outs, far_in=(), scratch=(), limit=8, far_out=False, cost=None):
    outs = [(o.shape, o.dtype) if hasattr(o, "shape") else o for o in outs]
    kind = (lambda s, t: jax.ShapeDtypeStruct(s, t)) if far_out else (lambda s, t: pltpu.VMEM(s, t))
    return pl.pallas_call(
        kernel,
        out_shape=tuple(kind(*o) for o in outs),
        in_specs=[NEAR] * len(near_in) + [FAR] * len(far_in),
        out_specs=tuple([NEAR] * len(outs)),
        scratch_shapes=list(scratch),
        compiler_params=pltpu.CompilerParams(vmem_limit_bytes=limit * MIB),
        cost_estimate=pl.CostEstimate(flops=cost or 0, bytes_accessed=cost or 0, transcendentals=0),
    )(*near(*near_in), *[pltpu.with_memory_space_constraint(a, pltpu.HBM) for a in far_in])


def shards(
    node_latent, fine_edges, fine_senders, fine_receivers, coarse_edges, coarse_senders,
    coarse_receivers, edge_weight_in, edge_bias, edge_weight_out, edge_gain, edge_shift,
    node_weight_in, node_bias, node_weight_out, node_gain, node_shift,
):
    nodes, d = node_latent.shape
    halo = nodes // 8
    block = halo + COARSE_DEV
    n_patches = lax.axis_size("wide")
    edges, coarse_count = fine_edges.shape[0], coarse_edges.shape[0]
    small = [node_latent] + [
        v.reshape(1, -1)
        for v in (
            fine_senders, fine_receivers, coarse_senders, coarse_receivers, edge_bias, node_bias,
            edge_gain, edge_shift, node_gain, node_shift,
        )
    ]
    dma = pltpu.SemaphoreType.DMA

    partner = lax.ppermute(node_latent, "narrow", [(0, 1), (1, 0)])
    nl, fs, fr, cs, cr, e_bias, n_bias, e_gain, e_shift, n_gain, n_shift = call(
        functools.partial(stage_kernel, len(small)), (), small,
        far_in=small + [fine_edges, edge_weight_in, node_weight_in], scratch=[dma((len(small),))], limit=1
    )
    (pay,) = call(functools.partial(pay_kernel, halo), (nl, partner), [((2 * block, d), BF16)], limit=1)
    around = range(n_patches)
    table_a = -(-2 * nodes // LANES) * LANES
    table_b = nodes + 4 * block
    base_c, oh1, oh2, sel, inc_f, inc_e, inc_l, pack, late, shifts, nu, table = call(
        functools.partial(local_kernel, nodes, halo, n_patches),
        (nl, fs, fr, cs, cr, e_bias, n_bias, e_shift, coarse_edges, edge_weight_in, node_weight_in),
        [
            ((coarse_count, d), F32),
            ((edges, table_a), BF16),
            ((edges, table_b), BF16),
            ((coarse_count, 2 * n_patches * COARSE_DEV), BF16),
            ((nodes, edges), BF16),
            ((nodes, edges), BF16),
            ((nodes, LATE + coarse_count), BF16),
            ((LATE, edges), BF16),
            ((8, LANES), F32),
            ((nodes, d), F32),
            ((nodes, d), F32),
            ((table_a, d), BF16),
        ],
        limit=16,
    )
    shift = lambda v, k: lax.ppermute(v, "wide", [(i, i ^ k) for i in around])
    x_rows = shift(pay, 1)
    known, rich = call(
        functools.partial(pair_kernel, halo), (pay, x_rows, base_c),
        [((4 * COARSE_DEV, d), BF16), ((4 * COARSE_DEV + 2 * halo, d), BF16)], limit=1,
    )
    (base_f,) = call(
        base_kernel,
        (oh1, table, edge_weight_in, e_bias, fine_edges, edge_weight_out, node_weight_out),
        [((edges, d), F32)],
        limit=16,
    )
    ready, hidden, part, pick = call(
        prep_kernel, (partner, x_rows, base_f, base_c, oh2, sel, pack, edge_weight_in),
        [
            ((table_b, d), BF16),
            ((edges, d), BF16),
            ((LATE + coarse_count, d), F32),
            ((LATE + coarse_count, LANES + sel.shape[1]), BF16),
        ],
        limit=12,
    )
    if n_patches == RING:
        spot = lambda p, c: p % n_patches * 2 + c
        split = lambda v, steps: lax.ppermute(
            v, ("wide", "narrow"),
            [(spot(p, c), spot(steps[c](p), c)) for p in around for c in range(2)],
        )
        first = split(rich, (lambda p: p + 2, lambda p: p - 2))
        second = split(known, (lambda p: p ^ 1, lambda p: p + 4))
        (both,) = call(
            both_kernel, (first, second, base_f, ready), [((8 * COARSE_DEV + 2 * halo, d), BF16)], limit=1
        )
        other = lax.ppermute(both, "narrow", [(0, 1), (1, 0)])
        far, picks = call(
            functools.partial(collect_kernel, halo), (known, both, other),
            [((2 * block, d), BF16), ((16 * COARSE_DEV, d), BF16)], limit=1,
        )
        pieces = (picks,)
    else:
        y_rows = lax.ppermute(
            pay, "wide", [(i, (i - 1 if i % 2 == 0 else i + 1) % n_patches) for i in around]
        )
        (far,) = call(
            functools.partial(wrap_kernel, halo), (y_rows,), [((2 * block, d), BF16)], limit=1
        )
        have = 2
        while True:
            pieces = [known]
            for k in range(1, min(4, n_patches // have)):
                pieces.append(shift(known, k * have))
            have *= len(pieces)
            if have == n_patches:
                break
            (known,) = call(
                join_kernel, pieces, [((len(pieces) * known.shape[0], d), BF16)], limit=2
            )
    coarse_rows = sum(p.shape[0] for p in pieces)

    (total,) = call(
        early_kernel, (hidden, inc_e, edge_weight_out), [((nodes, d), F32)],
        scratch=[pltpu.VMEM((edges, d), BF16)], limit=12,
    )
    (out,) = call(
        functools.partial(last_kernel, len(pieces)),
        (ready, far, nl, base_f, part, pick, oh2, inc_f, inc_l, late, total,
         shifts, nu, edge_weight_in, edge_weight_out, node_weight_in, node_weight_out,
         e_gain, n_gain, n_shift, *pieces),
        [((nodes, d), BF16)],
        scratch=[
            pltpu.VMEM((LANES + coarse_rows, d), BF16),
            pltpu.VMEM((table_b, d), BF16),
            pltpu.VMEM((edges, d), BF16),
            pltpu.VMEM((edges, d), BF16),
            pltpu.VMEM((nodes, d), F32),
        ],
        limit=16,
        far_out=True,
    )
    return out


def solution(mesh):
    axes = ("grp", "wide", "narrow")
    matrix, vector, whole = P(axes, None), P(axes), P()
    return jax.shard_map(
        shards,
        mesh=mesh,
        in_specs=(matrix, matrix, vector, vector, matrix, vector, vector) + (whole,) * 10,
        out_specs=matrix,
        check_vma=False,
    )
```

```python
import functools

import jax
import jax.numpy as jnp
from jax import lax
from jax.experimental import pallas as pl
from jax.experimental.pallas import tpu as pltpu
from jax.sharding import PartitionSpec as P


COARSE_DEV = 4
LANES = 128
CHUNKS = 3
LATE = 128
RING = 8
BF16 = jnp.bfloat16
F32 = jnp.float32
MIB = 1 << 20


def silu_of_half(u):
    return u + u * jnp.tanh(u)


def normalized(values):
    center = values - jnp.mean(values, axis=-1, keepdims=True)
    spread = jnp.mean(center * center, axis=-1, keepdims=True)
    return center * lax.rsqrt(spread + 1e-05)


def dot(a, b):
    return jnp.dot(a, b, preferred_element_type=F32)


def columns(row):
    return jnp.broadcast_to(row, (LANES, row.shape[1])).T


def one_hot(cols, width, value=1.0):
    lane = lax.broadcasted_iota(jnp.int32, cols[0].shape, 1)
    blocks = []
    for b in range(width // LANES):
        hit = cols[0] == lane + b * LANES
        for c in cols[1:]:
            hit = hit | (c == lane + b * LANES)
        blocks.append(jnp.where(hit, value, 0.0).astype(BF16))
    return jnp.concatenate(blocks, axis=1)


def stage_kernel(n, *refs):
    sems = refs[-1]
    copies = [pltpu.make_async_copy(refs[k], refs[k - n - 1], sems.at[k]) for k in range(n)]
    for c in copies:
        c.start()
    for c in copies:
        c.wait()


def pay_kernel(halo, nl, partner, pay):
    nodes = nl.shape[0]
    pick = lambda r: jnp.concatenate([r[nodes - halo :, :], r[:COARSE_DEV, :]], axis=0)
    own, other = pick(nl), pick(partner)
    low = lax.axis_index("narrow") == 0
    pay[...] = jnp.concatenate([jnp.where(low, own, other), jnp.where(low, other, own)], axis=0)


def coarse_of(rows, halo):
    block = halo + COARSE_DEV
    return [rows[halo:block, :], rows[block + halo : 2 * block, :]]


def pair_kernel(halo, pay, x_rows, _, known, rich):
    known[...] = jnp.concatenate(coarse_of(pay, halo) + coarse_of(x_rows, halo), axis=0)
    rich[...] = jnp.concatenate([known[...]] + halos_of(x_rows, halo), axis=0)


def both_kernel(first, second, _, __, both):
    n = first.shape[0]
    both[:n, :] = first[...]
    both[n:, :] = second[...]


def halos_of(rows, halo):
    block = halo + COARSE_DEV
    return [rows[:halo, :], rows[block : block + halo, :]]


def collect_kernel(halo, known, both, other, far, picks):
    n, m = 2 * halo, known.shape[0]
    low = lax.axis_index("narrow") == 0
    even = lax.axis_index("wide") % 2 == 0
    zero, one = jnp.where(low, both[...], other[...]), jnp.where(low, other[...], both[...])
    picks[...] = jnp.concatenate([known[...], one[:m], one[m + n :], zero[:m]], axis=0)
    source = jnp.where(even, zero[m : m + n], one[m : m + n])
    far[...] = jnp.concatenate([source, known[: 2 * COARSE_DEV]], axis=0)


def wrap_kernel(halo, y_rows, far):
    far[...] = jnp.concatenate(
        halos_of(y_rows[...], halo) + [y_rows[: 2 * COARSE_DEV, :]], axis=0
    )


def join_kernel(*refs):
    at = 0
    for r in refs[:-1]:
        refs[-1][at : at + r.shape[0], :] = r[...]
        at += r.shape[0]


def places(n_patches):
    wide = lax.axis_index("wide")
    half = lax.axis_index("narrow")
    y_patch = jnp.where(wide % 2 == 0, wide + n_patches - 1, wide + 1) % n_patches
    return wide, half, wide * 2 + half, y_patch


def local_kernel(
    nodes, halo, n_patches,
    nl, fs, fr, cs, cr, e_bias, n_bias, e_shift, ce, w_in, u_in,
    base_c, oh1, oh2, sel, inc_f, inc_e, inc_l, pack, late, shifts, nu, table,
):
    d = nl.shape[1]
    wide, half, device, y_patch = places(n_patches)
    patch = 2 * nodes
    first = nodes - halo
    block = halo + COARSE_DEV

    recv = fr[...] - device * nodes
    send = fs[...]

    def offset(p):
        off = send - p * patch
        inside = (off >= 0) & (off < patch)
        upper = (off >= nodes).astype(jnp.int32)
        return inside, upper, off - upper * nodes

    inside, upper, loc = offset(wide)
    own = jnp.where(inside & (upper == half), loc + nodes, -1)
    pos = jnp.where(inside & (upper != half), loc, -1)
    for k, p in enumerate((wide ^ 1, y_patch)):
        inside, upper, loc = offset(p)
        at = nodes + k * 2 * block + upper * (block, halo)[k] + loc - first
        pos = jnp.where(inside, at, pos)

    recv_c = cr[...] - device * nodes
    chip_rows = cs[...].astype(F32)
    owner = jnp.floor((chip_rows + 0.5) * (1.0 / nodes)).astype(jnp.int32)
    slot_c = cs[...] - owner * nodes
    patch_c = owner // 2
    if n_patches == RING:
        pairs = n_patches // 2
        place_c = (patch_c // 2 - wide // 2 + pairs) % pairs * 2 + (patch_c ^ wide) % 2
    else:
        place_c = patch_c ^ wide
    pos_c = place_c * (2 * COARSE_DEV) + (owner % 2) * COARSE_DEV + slot_c

    def incidence(ids):
        at = lax.broadcasted_iota(jnp.int32, (nodes, ids.shape[1]), 0)
        return jnp.where(at == ids, 1.0, 0.0)

    edges = fr.shape[1]
    last_block = pos >= nodes + 2 * block
    late_row = jnp.where(last_block, 1.0, 0.0)
    before = lax.broadcasted_iota(jnp.int32, (edges, edges), 0)
    before = before < lax.broadcasted_iota(jnp.int32, (edges, edges), 1)
    flags = jnp.broadcast_to(late_row, (8, edges)).astype(BF16)
    rank = dot(flags, jnp.where(before, 1.0, 0.0).astype(BF16))[0:1, :].astype(jnp.int32)
    rank = jnp.where(last_block, rank, -1)
    chosen = lax.broadcasted_iota(jnp.int32, pack.shape, 0) == rank
    chosen = jnp.where(chosen, 1.0, 0.0).astype(BF16)
    pack[...] = chosen
    late[...] = late_row
    marks, marks_c = incidence(recv), incidence(recv_c)
    inc_f[...] = marks.astype(BF16)
    inc_e[...] = (marks * (1.0 - late_row)).astype(BF16)
    inc_l[:, :LATE] = lax.dot_general(
        marks.astype(BF16), chosen, (((1,), (1,)), ((), ())), preferred_element_type=F32
    ).astype(BF16)
    inc_l[:, LATE:] = marks_c.astype(BF16)
    count = jnp.sum(marks, axis=1, keepdims=True) + jnp.sum(marks_c, axis=1, keepdims=True)
    shifts[...] = count * e_shift[...]
    wide_c = -(-sel.shape[1] // LANES) * LANES
    sel[...] = one_hot((columns(pos_c),), wide_c, 0.5)[:, : sel.shape[1]]
    oh_c = one_hot((columns(recv_c),), table.shape[0])
    oh1[...] = one_hot((columns(recv), columns(own)), oh1.shape[1], 0.5)
    oh2[...] = one_hot((columns(pos),), oh2.shape[1], 0.5)
    table[2 * nodes :, :] = jnp.zeros_like(table[2 * nodes :, :])

    node_rows = nl[...]
    table[0:nodes, :] = dot(node_rows, w_in[2 * d :, :]).astype(BF16)
    table[nodes : 2 * nodes, :] = dot(node_rows, w_in[d : 2 * d, :]).astype(BF16)
    nu[...] = 0.5 * (dot(node_rows, u_in[:d, :]) + n_bias[...])
    base_c[...] = 0.5 * (dot(ce[...], w_in[:d, :]) + dot(oh_c, table[...]) + e_bias[...])


def base_kernel(oh1, table, w_in, e_bias, fe, _, __, base_f):
    d = fe.shape[1]
    own = 0.5 * (dot(fe[...], w_in[:d, :]) + e_bias[...])
    base_f[...] = own + dot(oh1[...], table[...])


def w_send(w_in):
    d = w_in.shape[1]
    return w_in[d : 2 * d, :]


def prep_kernel(partner, x_rows, base_f, base_c, oh2, sel, pack, w_in, ready, hidden, part, pick):
    n = partner.shape[0]
    m = n + x_rows.shape[0]
    ready[:n, :] = dot(partner[...], w_send(w_in)).astype(BF16)
    ready[n:m, :] = dot(x_rows[...], w_send(w_in)).astype(BF16)
    ready[m:, :] = jnp.zeros_like(ready[m:, :])
    half = base_f[...]
    hidden[...] = silu_of_half(half + dot(oh2[...], ready[...])).astype(BF16)
    coarse_bits = half.astype(BF16)
    fine_bits = (half - coarse_bits.astype(F32)).astype(BF16)
    late = pack.shape[0]
    part[:late, :] = dot(pack[...], coarse_bits)
    part[late:, :] = base_c[...]
    pick[...] = jnp.zeros_like(pick)
    pick[:late, :LANES] = dot(pack[...], oh2[:, oh2.shape[1] - LANES :]).astype(BF16)
    pick[late:, LANES:] = sel[...]


def early_kernel(hidden, inc_e, w_out, total, mess):
    rows = hidden.shape[0]
    step = rows // CHUNKS
    for k in range(CHUNKS):
        s = slice(k * step, (k + 1) * step)
        mess[s, :] = normalized(dot(hidden[s, :], w_out[...])).astype(BF16)
    total[...] = dot(inc_e[...], mess[...])


def last_kernel(
    n_pieces, ready, far, nl, base_f, part, pick, oh2, inc_f, inc_l, late,
    total, shifts, nu, w_in, w_out, u_in, u_out, e_gain, n_gain, n_shift, *refs,
):
    pieces, (out, rows, table, hidden, mess, acc) = refs[:n_pieces], refs[n_pieces:]
    w_s = w_send(w_in)
    a = LANES - far.shape[0]
    rows[:a, :] = jnp.zeros_like(rows[:a, :])
    rows[a:LANES, :] = far[...]
    rows[LANES:, :] = jnp.concatenate([r[...] for r in pieces], axis=0)
    picked = dot(pick[...], rows[...]).astype(BF16)
    half = part[...] + dot(picked, w_s)
    some = normalized(dot(silu_of_half(half).astype(BF16), w_out[...])).astype(BF16)
    acc[...] = total[...] + dot(inc_l[...], some)

    @pl.when(jnp.sum(late[...]) > LATE)
    def _():
        a = ready.shape[0] - far.shape[0]
        table[:a, :] = ready[:a, :]
        table[a:, :] = dot(far[...], w_s).astype(BF16)
        step = base_f.shape[0] // CHUNKS
        for k in range(CHUNKS):
            s = slice(k * step, (k + 1) * step)
            hidden[s, :] = silu_of_half(base_f[s, :] + dot(oh2[s, :], table[...])).astype(BF16)
            mess[s, :] = normalized(dot(hidden[s, :], w_out[...])).astype(BF16)
        acc[...] = dot(inc_f[...], mess[...]) + dot(inc_l[:, LATE:], some[LATE:])

    summed = acc[...] * e_gain[...] + shifts[...]
    d = nl.shape[1]
    half = nu[...] + 0.5 * dot(summed.astype(BF16), u_in[d:, :])
    update = normalized(dot(silu_of_half(half).astype(BF16), u_out[...]))
    out[...] = (nl[...].astype(F32) + (update * n_gain[...] + n_shift[...])).astype(BF16)


NEAR = pl.BlockSpec(memory_space=pltpu.VMEM)
FAR = pl.BlockSpec(memory_space=pltpu.HBM)


def near(*arrays):
    return [pltpu.with_memory_space_constraint(a, pltpu.VMEM) for a in arrays]


def call(kernel, near_in, outs, far_in=(), scratch=(), limit=8, far_out=False, cost=None):
    outs = [(o.shape, o.dtype) if hasattr(o, "shape") else o for o in outs]
    kind = (lambda s, t: jax.ShapeDtypeStruct(s, t)) if far_out else (lambda s, t: pltpu.VMEM(s, t))
    return pl.pallas_call(
        kernel,
        out_shape=tuple(kind(*o) for o in outs),
        in_specs=[NEAR] * len(near_in) + [FAR] * len(far_in),
        out_specs=tuple([NEAR] * len(outs)),
        scratch_shapes=list(scratch),
        compiler_params=pltpu.CompilerParams(vmem_limit_bytes=limit * MIB),
        cost_estimate=pl.CostEstimate(flops=cost or 0, bytes_accessed=cost or 0, transcendentals=0),
    )(*near(*near_in), *[pltpu.with_memory_space_constraint(a, pltpu.HBM) for a in far_in])


def shards(
    node_latent, fine_edges, fine_senders, fine_receivers, coarse_edges, coarse_senders,
    coarse_receivers, edge_weight_in, edge_bias, edge_weight_out, edge_gain, edge_shift,
    node_weight_in, node_bias, node_weight_out, node_gain, node_shift,
):
    nodes, d = node_latent.shape
    halo = nodes // 8
    block = halo + COARSE_DEV
    n_patches = lax.axis_size("wide")
    edges, coarse_count = fine_edges.shape[0], coarse_edges.shape[0]
    small = [node_latent] + [
        v.reshape(1, -1)
        for v in (
            fine_senders, fine_receivers, coarse_senders, coarse_receivers, edge_bias, node_bias,
            edge_gain, edge_shift, node_gain, node_shift,
        )
    ]
    dma = pltpu.SemaphoreType.DMA

    partner = lax.ppermute(node_latent, "narrow", [(0, 1), (1, 0)])
    nl, fs, fr, cs, cr, e_bias, n_bias, e_gain, e_shift, n_gain, n_shift = call(
        functools.partial(stage_kernel, len(small)), (), small,
        far_in=small + [fine_edges, edge_weight_in, node_weight_in], scratch=[dma((len(small),))], limit=1
    )
    (pay,) = call(functools.partial(pay_kernel, halo), (nl, partner), [((2 * block, d), BF16)], limit=1)
    around = range(n_patches)
    table_a = -(-2 * nodes // LANES) * LANES
    table_b = nodes + 4 * block
    base_c, oh1, oh2, sel, inc_f, inc_e, inc_l, pack, late, shifts, nu, table = call(
        functools.partial(local_kernel, nodes, halo, n_patches),
        (nl, fs, fr, cs, cr, e_bias, n_bias, e_shift, coarse_edges, edge_weight_in, node_weight_in),
        [
            ((coarse_count, d), F32),
            ((edges, table_a), BF16),
            ((edges, table_b), BF16),
            ((coarse_count, 2 * n_patches * COARSE_DEV), BF16),
            ((nodes, edges), BF16),
            ((nodes, edges), BF16),
            ((nodes, LATE + coarse_count), BF16),
            ((LATE, edges), BF16),
            ((1, edges), F32),
            ((nodes, d), F32),
            ((nodes, d), F32),
            ((table_a, d), BF16),
        ],
        limit=16,
    )
    shift = lambda v, k: lax.ppermute(v, "wide", [(i, i ^ k) for i in around])
    x_rows = shift(pay, 1)
    known, rich = call(
        functools.partial(pair_kernel, halo), (pay, x_rows, base_c),
        [((4 * COARSE_DEV, d), BF16), ((4 * COARSE_DEV + 2 * halo, d), BF16)], limit=1,
    )
    (base_f,) = call(
        base_kernel,
        (oh1, table, edge_weight_in, e_bias, fine_edges, edge_weight_out, node_weight_out),
        [((edges, d), F32)],
        limit=16,
    )
    ready, hidden, part, pick = call(
        prep_kernel, (partner, x_rows, base_f, base_c, oh2, sel, pack, edge_weight_in),
        [
            ((table_b, d), BF16),
            ((edges, d), BF16),
            ((LATE + coarse_count, d), F32),
            ((LATE + coarse_count, LANES + sel.shape[1]), BF16),
        ],
        limit=12,
    )
    if n_patches == RING:
        spot = lambda p, c: p % n_patches * 2 + c
        split = lambda v, steps: lax.ppermute(
            v, ("wide", "narrow"),
            [(spot(p, c), spot(steps[c](p), c)) for p in around for c in range(2)],
        )
        first = split(rich, (lambda p: p + 2, lambda p: p - 2))
        second = split(known, (lambda p: p ^ 1, lambda p: p + 4))
        (both,) = call(
            both_kernel, (first, second, base_f, ready), [((8 * COARSE_DEV + 2 * halo, d), BF16)], limit=1
        )
        other = lax.ppermute(both, "narrow", [(0, 1), (1, 0)])
        far, picks = call(
            functools.partial(collect_kernel, halo), (known, both, other),
            [((2 * block, d), BF16), ((16 * COARSE_DEV, d), BF16)], limit=1,
        )
        pieces = (picks,)
    else:
        y_rows = lax.ppermute(
            pay, "wide", [(i, (i - 1 if i % 2 == 0 else i + 1) % n_patches) for i in around]
        )
        (far,) = call(
            functools.partial(wrap_kernel, halo), (y_rows,), [((2 * block, d), BF16)], limit=1
        )
        have = 2
        while True:
            pieces = [known]
            for k in range(1, min(4, n_patches // have)):
                pieces.append(shift(known, k * have))
            have *= len(pieces)
            if have == n_patches:
                break
            (known,) = call(
                join_kernel, pieces, [((len(pieces) * known.shape[0], d), BF16)], limit=2
            )
    coarse_rows = sum(p.shape[0] for p in pieces)

    (total,) = call(
        early_kernel, (hidden, inc_e, edge_weight_out), [((nodes, d), F32)],
        scratch=[pltpu.VMEM((edges, d), BF16)], limit=12,
    )
    (out,) = call(
        functools.partial(last_kernel, len(pieces)),
        (ready, far, nl, base_f, part, pick, oh2, inc_f, inc_l, late, total,
         shifts, nu, edge_weight_in, edge_weight_out, node_weight_in, node_weight_out,
         e_gain, n_gain, n_shift, *pieces),
        [((nodes, d), BF16)],
        scratch=[
            pltpu.VMEM((LANES + coarse_rows, d), BF16),
            pltpu.VMEM((table_b, d), BF16),
            pltpu.VMEM((edges, d), BF16),
            pltpu.VMEM((edges, d), BF16),
            pltpu.VMEM((nodes, d), F32),
        ],
        limit=16,
        far_out=True,
    )
    return out


def solution(mesh):
    axes = ("grp", "wide", "narrow")
    matrix, vector, whole = P(axes, None), P(axes), P()
    return jax.shard_map(
        shards,
        mesh=mesh,
        in_specs=(matrix, matrix, vector, vector, matrix, vector, vector) + (whole,) * 10,
        out_specs=matrix,
        check_vma=False,
    )
```
